128 devices in a mesh: board: 32 (over x, y, core), hand: 4 (over z).
Axes of the slice: x: 4, y: 4, z: 4, core: 2. Of those that a mesh axis runs over, the one named last changes fastest.
Arguments:
- reach_pre: float32 [1408], P(('board', 'hand')), may hold values from 0.05 to 1
- strategy: bfloat16 [256, 128, 1408], P('board', None, 'hand'), may hold values from 0 to 1
- ranks: int32 [256, 8, 1408], P('board'), may hold values from 0 to 94
- boards: int32 [256, 8, 5], P('board'), may hold values from 0 to 51, as said below
- river_live: int32 [256], P('board'), may hold values from 1 to 8, as said below
- iso_weight: int32 [256], P('board'), may hold values from 1 to 24
- pot: float32 [128], replicated, may hold values from 2 to 24
- line_act: int32 [128], replicated, may hold values from 0 to 2
Outputs:
- preflop_value: float32 [1408], P('hand')
The draws below stay inside these ranges and needn't reach their ends.
Inputs may be any that keep to these rules, and one draw needn't show every extreme that they name: `boards`: the five cards of a runout are distinct; all runouts of a flop share their first three cards. `river_live`: in every draw some flop has all 8 runouts live.
All inputs are finite; a program needn't handle non-finite values.
Results may differ from the reference program's by a relative error of at most 0.0003.
Values may be sent and summed in bfloat16 or wider, within the bound.
A program may use at most 64 MiB of HBM per device.

```python
import math
import jax
import jax.numpy as jnp
import numpy as np
from jax import lax

HANDS = 1326
HPAD = 1408
RIV = 8
LINES = 128
ACTS = 3
FLOPS = 256


def draw_ranks(key, part):
    base_rank = jax.random.randint(jax.random.fold_in(key, 11), (1, 1, HPAD), 0, 32)
    noise_rank = jax.random.randint(jax.random.fold_in(key, 12), (FLOPS, RIV, HPAD), 0, 64)
    drawn = (base_rank + noise_rank).astype(jnp.int32)
    entries = FLOPS * RIV * HPAD
    position = jnp.arange(entries, dtype=jnp.int32).reshape(FLOPS, RIV, HPAD)
    low_at = jax.random.randint(jax.random.fold_in(key, 13), (), 0, entries)
    high_at = (low_at + 1 + jax.random.randint(jax.random.fold_in(key, 14), (), 0, entries - 1)) % entries
    drawn = jnp.where(position == low_at, 0, drawn)
    drawn = jnp.where(position == high_at, 94, drawn)
    return drawn.astype(jnp.int32)


def draw_boards(key, part):
    scores = jax.random.randint(jax.random.fold_in(key, 21), (FLOPS, 52), 0, 1 << 20) * 64 + jnp.arange(52, dtype=jnp.int32)[None, :]
    order = jnp.argsort(scores, axis=1).astype(jnp.int32)
    flop_cards = jnp.broadcast_to(order[:, None, 0:3], (FLOPS, RIV, 3))
    turn_cards = order[:, 3:3 + 2 * RIV:2]
    river_cards = order[:, 4:4 + 2 * RIV:2]
    return jnp.concatenate([flop_cards, turn_cards[:, :, None], river_cards[:, :, None]], axis=2).astype(jnp.int32)


def draw_river_live(key, part):
    heavy = jax.random.randint(jax.random.fold_in(key, 31), (FLOPS,), 0, 3) == 0
    counts = jax.random.randint(jax.random.fold_in(key, 32), (FLOPS,), 1, RIV + 1)
    counts = jnp.where(heavy, counts, 1)
    chosen = jax.random.randint(jax.random.fold_in(key, 33), (), 0, FLOPS)
    return jnp.where(jnp.arange(FLOPS, dtype=jnp.int32) == chosen, RIV, counts).astype(jnp.int32)


def set_ends(values, rng, smallest, high):
    dims = values.shape
    place = [jax.random.randint(jax.random.fold_in(rng, axis), (), 0, dims[axis]) for axis in range(len(dims))]
    values = values.at[tuple(place)].set(smallest)
    longest = dims.index(max(dims))
    place[longest] = (place[longest] + 1) % dims[longest]
    return values.at[tuple(place)].set(high)


def steps_of(stream_key, shape, shards, least, top_value):
    gain, own = 1.0, jax.random.fold_in(stream_key, 6)
    for dim, parts in shards:
        steps = jnp.exp(jax.random.uniform(jax.random.fold_in(own, dim), (parts,), jnp.float32, least / len(shards), top_value / len(shards)))
        gain = gain * jnp.repeat(steps, shape[dim] // parts).reshape([-1 if axis == dim else 1 for axis in range(len(shape))])
    return gain


def setup_inputs(seed: int = 0) -> dict:
    seeds = jax.random.split(jax.random.key(seed), 9)
    reach_pre = jnp.clip(jnp.exp(math.log(1.0) - 2.9957323 * jax.random.uniform(seeds[0], (HPAD,), jnp.float32) ** steps_of(seeds[0], (HPAD,), ((0, 128),), -0.2, 0.2)), 0.05, 1.0)
    strategy = jnp.clip(1.0 * jax.random.uniform(seeds[1], (FLOPS, LINES, HPAD), jnp.float32) ** steps_of(seeds[1], (FLOPS, LINES, HPAD), ((0, 32), (2, 4)), -0.2, 0.2), 0.0, 1.0).astype(jnp.bfloat16)
    ranks = draw_ranks(jax.random.fold_in(seeds[8], 71), 0)
    boards = draw_boards(jax.random.fold_in(seeds[8], 71), 0)
    river_live = draw_river_live(jax.random.fold_in(seeds[8], 71), 0)
    iso_weight = set_ends(jax.random.randint(seeds[5], (FLOPS,), 1, 25), jax.random.fold_in(seeds[5], 1), 1, 24).astype(jnp.int32)
    pot = jnp.clip(jnp.exp(jax.random.uniform(seeds[6], (LINES,), jnp.float32, math.log(2.0), math.log(24.0))), 2.0, 24.0)
    line_act = set_ends(jax.random.randint(seeds[7], (LINES,), 0, ACTS), jax.random.fold_in(seeds[7], 1), 0, ACTS - 1).astype(jnp.int32)
    return dict(reach_pre=reach_pre, strategy=strategy, ranks=ranks, boards=boards, river_live=river_live, iso_weight=iso_weight, pot=pot, line_act=line_act)


def card_tables():
    first_card, second_card = np.triu_indices(52, 1)
    padding = HPAD - HANDS
    first_card = np.concatenate([first_card, np.full(padding, 52)]).astype(np.int32)
    second_card = np.concatenate([second_card, np.full(padding, 53)]).astype(np.int32)
    alive_mask = np.concatenate([np.ones(HANDS), np.zeros(padding)]).astype(np.float32)
    return jnp.asarray(first_card), jnp.asarray(second_card), jnp.asarray(alive_mask)


def unblocked(first_rows, second_rows, first_cols, second_cols):
    clear = (first_rows[:, None] != first_cols[None, :]) & (first_rows[:, None] != second_cols[None, :])
    clear = clear & (second_rows[:, None] != first_cols[None, :]) & (second_rows[:, None] != second_cols[None, :])
    return clear.astype(jnp.float32)


def live_hands(first_card, second_card, alive_mask, board_cards):
    clear = jnp.all((first_card[:, None] != board_cards[None, :]) & (second_card[:, None] != board_cards[None, :]), axis=1)
    return alive_mask * clear.astype(jnp.float32)


def showdown(rank_rows, rank_cols, live_rows, live_cols, blocking):
    signed = jnp.sign(rank_rows[:, None] - rank_cols[None, :]).astype(jnp.float32)
    return (signed * blocking.astype(jnp.float32) * live_rows[:, None] * live_cols[None, :]).astype(jnp.bfloat16)


def reference(reach_pre, strategy, ranks, boards, river_live, iso_weight, pot, line_act):
    first_card, second_card, alive_mask = card_tables()
    total_reach = jnp.sum(reach_pre * alive_mask)
    blocking = unblocked(first_card, second_card, first_card, second_card).astype(jnp.bfloat16)
    onehot = (line_act[:, None] == jnp.arange(ACTS, dtype=jnp.int32)[None, :]).astype(jnp.float32)

    def per_flop(running, items):
        strat_flop, ranks_flop, boards_flop, count_flop, iso_flop = items
        line_reach = (reach_pre[None, :] * strat_flop.astype(jnp.float32) / total_reach).astype(jnp.bfloat16)

        def one_runout(runout, acc):
            live_now = live_hands(first_card, second_card, alive_mask, boards_flop[runout])
            matrix = showdown(ranks_flop[runout], ranks_flop[runout], live_now, live_now, blocking)
            values = jnp.dot(matrix, line_reach.T, preferred_element_type=jnp.float32)
            return acc + values * (runout < count_flop).astype(jnp.float32)

        acc = lax.fori_loop(0, RIV, one_runout, jnp.zeros((HPAD, LINES), jnp.float32))
        line_values = acc * pot[None, :] / count_flop.astype(jnp.float32)
        group_values = jnp.dot(line_values, onehot, precision=lax.Precision.HIGHEST, preferred_element_type=jnp.float32)
        best = jnp.max(group_values, axis=1)
        return running + iso_flop.astype(jnp.float32) * best, None

    summed, unused = lax.scan(per_flop, jnp.zeros((HPAD,), jnp.float32), (strategy, ranks, boards, river_live, iso_weight))
    return summed / jnp.sum(iso_weight.astype(jnp.float32))
```

```python
import functools

import jax
import jax.numpy as jnp
import numpy as np
from jax import lax
from jax.experimental import pallas as pl
from jax.experimental.pallas import tpu as pltpu
from jax.sharding import PartitionSpec as P

HANDS = 1326
HPAD = 1408
RIV = 8
LINES = 128
ACTS = 3
NF = 8
OWN = 352
OPAD = 384
CHUNK = 11
DEAD = 128.0
XS, YS, CS, ZS = 4, 4, 2, 4
NB = XS * YS * CS
PARTS = 3
ROWS = PARTS * ACTS * NF
RPAD = 80
f32, bf16 = jnp.float32, jnp.bfloat16


def card_rows():
    first, second = np.triu_indices(52, 1)
    padding = HPAD - HANDS
    rows = np.zeros((8, HPAD), np.float32)
    rows[0] = np.concatenate([first, np.full(padding, 52)])
    rows[1] = np.concatenate([second, np.full(padding, 53)])
    rows[2] = np.arange(HPAD) < HANDS
    return rows


def pieces(value):
    high = value.astype(bf16)
    rest = value - high.astype(f32)
    middle = rest.astype(bf16)
    low = (rest - middle.astype(f32)).astype(bf16)
    return high, middle, low


def kernel(
    reach_hbm, strategy_hbm, ranks_hbm, boards_hbm, pot_hbm, act_hbm, cards_hbm, live_smem, iso_smem,
    out_ref,
    reach_in, strat, ranks, boards, pot, act, cards,
    rk, rows_b, cols_b, dead_j, block, mat, sel, pick, wslot, wall, rhs, gathered, final,
    load_sem, s1, r1, s2, r2, s3, r3, s4, r4, s5, r5,
):
    board, hand = lax.axis_index("board"), lax.axis_index("hand")
    x, y, core = board // (YS * CS), (board // CS) % YS, board % CS

    def board_of(xx, yy, cc):
        return (xx * YS + yy) * CS + cc

    near = [(dz, dc) for dz in range(ZS) for dc in range(CS) if dz or dc]

    barrier = pltpu.get_barrier_semaphore()

    def greet(b, h):
        pl.semaphore_signal(barrier, inc=1, device_id=(b, h), device_id_type=pl.DeviceIdType.MESH)

    for dz, dc in near:
        greet(board_of(x, y, (core + dc) % CS), (hand + dz) % ZS)
    for k in range(1, YS):
        greet(board_of(x, (y + k) % YS, core), hand)
    for k in range(1, XS):
        greet(board_of((x + k) % XS, y, core), hand)

    loads = [
        pltpu.make_async_copy(a, b, load_sem.at[i])
        for i, (a, b) in enumerate(
            [(reach_hbm, reach_in), (cards_hbm, cards), (boards_hbm, boards), (ranks_hbm, ranks),
             (pot_hbm, pot), (act_hbm, act), (strategy_hbm, strat)]
        )
    ]
    for c in loads:
        c.start()
    loads[0].wait()
    mine = board * ZS + hand
    gathered[pl.ds(mine, 1), 0:1, 0:CHUNK] = reach_in[...].reshape(1, 1, CHUNK)
    for c in loads[1:6]:
        c.wait()

    c1, c2, alive = cards[0:1, :], cards[1:2, :], cards[2:3, :]
    runout = lax.broadcasted_iota(jnp.int32, (RIV, 1), 0)
    for f in range(NF):
        cols = boards[f].astype(f32)
        dead = jnp.broadcast_to(alive < 0.5, (RIV, HPAD))
        for k in range(5):
            card = cols[:, k : k + 1]
            dead = dead | (c1 == card) | (c2 == card)
        dead = dead | (runout >= live_smem[f])
        here = jnp.where(dead, DEAD, ranks[f].astype(f32))
        rk[RIV * f : RIV * (f + 1), :] = here
        rk[64 + f : 65 + f, :] = jnp.sum(dead.astype(f32), axis=0, keepdims=True)
    rk[72:74, :] = cards[0:2, :]
    rk[74:80, :] = jnp.zeros((6, HPAD), f32)

    own = rk[:, 0:OPAD]
    for z in range(1, ZS):
        if z < ZS - 1:
            part = rk[:, OWN * z : OWN * z + OPAD]
        else:
            part = jnp.concatenate([rk[:, OWN * z :], jnp.zeros((80, OPAD - OWN), f32)], axis=1)
        own = jnp.where(hand == z, part, own)
    own = jnp.concatenate([own, jnp.zeros((48, OPAD), f32)], axis=0)
    columns = own.T[0:OWN, :]
    for q in range(74):
        cols_b[q] = jnp.broadcast_to(columns[:, q : q + 1], (OWN, 128)).astype(bf16)
    for q in range(74):
        rows_b[q] = jnp.broadcast_to(rk[q : q + 1, :], (16, HPAD)).astype(bf16)

    def spread(row):
        return jnp.broadcast_to(row[None], (OWN // 16, 16, 128)).reshape(OWN, 128)

    one = jnp.ones((), bf16)

    def tile_of_block(t, carry):
        at = pl.ds(pl.multiple_of(t * 128, 128), 128)
        a1, a2 = cols_b[72], cols_b[73]
        b1, b2 = spread(rows_b[72, :, at]), spread(rows_b[73, :, at])
        product = ((a1 - b1) * (a1 - b2)) * ((a2 - b1) * (a2 - b2))
        block[:, at] = jnp.minimum(jnp.abs(product), one)
        return carry

    lax.fori_loop(0, HPAD // 128, tile_of_block, 0)

    def build(lo, hi):
        def step(i, carry):
            f, t = i // (HPAD // 128), i % (HPAD // 128)
            at = pl.ds(pl.multiple_of(t * 128, 128), 128)
            acc = spread(rows_b[64 + f, :, at]) - cols_b[64 + f]
            for r in range(RIV):
                gap = cols_b[RIV * f + r] - spread(rows_b[RIV * f + r, :, at])
                acc = acc + jnp.maximum(jnp.minimum(gap, one), -one)
            mat[:, pl.ds(pl.multiple_of(f * HPAD + t * 128, 128), 128)] = acc * block[:, at]
            return carry

        lax.fori_loop(lo * (HPAD // 128), hi * (HPAD // 128), step, 0)

    flop_of_row = lax.broadcasted_iota(jnp.int32, (NF, 128), 0)
    pot_row, act_row = pot[...].reshape(1, LINES), act[...].reshape(1, LINES)
    weights = [pieces(jnp.where(act_row == a, pot_row, 0.0)) for a in range(ACTS)]
    for f in range(NF):
        groups = [
            jnp.where(flop_of_row == f, jnp.broadcast_to(weights[a][p].astype(f32), (NF, LINES)), 0.0)
            for p in range(PARTS) for a in range(ACTS)
        ] + [jnp.zeros((NF, LINES), f32)]
        sel[:, LINES * f : LINES * (f + 1)] = jnp.concatenate(groups, axis=0).astype(bf16)

    pl.semaphore_wait(barrier, len(near) + YS - 1 + XS - 1)

    def remote(src, dst, send, recv, b, h):
        return pltpu.make_async_remote_copy(
            src_ref=src, dst_ref=dst, send_sem=send, recv_sem=recv,
            device_id=(b, h), device_id_type=pl.DeviceIdType.MESH,
        )

    row = gathered.at[pl.ds(mine, 1)]
    first = [
        remote(row, row, s1.at[i], r1.at[i], board_of(x, y, (core + dc) % CS), (hand + dz) % ZS)
        for i, (dz, dc) in enumerate(near)
    ]
    for c in first:
        c.start()
    build(0, 2)
    for c in first:
        c.wait_recv()
    group = gathered.at[pl.ds((x * YS + y) * 8, 8)]
    second = [
        remote(group, group, s2.at[k - 1], r2.at[k - 1], board_of(x, (y + k) % YS, core), hand)
        for k in range(1, YS)
    ]
    for c in second:
        c.start()
    build(2, 4)
    for c in second:
        c.wait_recv()
    plane = gathered.at[pl.ds(x * 32, 32)]
    third = [
        remote(plane, plane, s3.at[k - 1], r3.at[k - 1], board_of((x + k) % XS, y, core), hand)
        for k in range(1, XS)
    ]
    for c in third:
        c.start()
    build(4, 6)
    loads[6].wait()
    for c in third:
        c.wait_recv()

    every = gathered[:, 0, :]
    entry = lax.broadcasted_iota(jnp.int32, (128, 128), 0) * CHUNK + lax.broadcasted_iota(jnp.int32, (128, 128), 1)
    lane = lax.broadcasted_iota(jnp.int32, (128, 128), 1)
    every = jnp.where(lane < CHUNK, every, 0.0)
    total = jnp.sum(jnp.where(entry < HANDS, every, 0.0))
    quarter = every[0:32]
    for z in range(1, ZS):
        quarter = jnp.where(hand == z, every[32 * z : 32 * (z + 1)], quarter)
    stacked = jnp.concatenate([p.astype(f32) for p in pieces(quarter)], axis=0).astype(bf16)
    hand_at = lax.broadcasted_iota(jnp.int32, (128, OPAD), 1)
    spot = (hand_at - (hand_at // CHUNK) * CHUNK) == lax.broadcasted_iota(jnp.int32, (128, OPAD), 0)
    laid = jnp.dot(stacked, spot.astype(f32).astype(bf16), preferred_element_type=f32)
    laid = laid[0:32] + laid[32:64] + laid[64:96]
    owner = lax.broadcasted_iota(jnp.int32, (32, OPAD), 1) // CHUNK
    laid = jnp.where(owner == lax.broadcasted_iota(jnp.int32, (32, OPAD), 0), laid, 0.0)
    share = (jnp.sum(laid, axis=0, keepdims=True) / total)[:, 0:OWN]

    lines = (strat[...].reshape(NF * LINES, OWN).astype(f32) * share).astype(bf16)
    summed = jnp.dot(sel[...], lines, preferred_element_type=f32)
    wslot[pl.ds(hand, 1), :, 0:OWN] = (summed[0:24] + summed[24:48] + summed[48:72])[None]
    held = wslot.at[pl.ds(hand, 1)]
    fourth = [
        remote(held, held, s4.at[k - 1], r4.at[k - 1], board, (hand + k) % ZS) for k in range(1, ZS)
    ]
    for c in fourth:
        c.start()
    build(6, 8)
    for c in fourth:
        c.wait_recv()

    for z in range(ZS):
        wall[:, OWN * z : OWN * (z + 1)] = wslot[z, :, 0:OWN]
    cut = [p.astype(f32) for p in pieces(wall[...])]
    flop_of_lane = lax.broadcasted_iota(jnp.int32, (NF, HPAD), 0)
    values = jnp.zeros((OWN, RPAD), f32)
    for f in range(NF):
        groups = [
            jnp.where(flop_of_lane == f, cut[p][NF * a : NF * (a + 1)], 0.0)
            for p in range(PARTS) for a in range(ACTS)
        ] + [jnp.zeros((NF, HPAD), f32)]
        right = jnp.concatenate(groups, axis=0).astype(bf16)
        values += lax.dot_general(
            mat[:, HPAD * f : HPAD * (f + 1)], right, (((1,), (1,)), ((), ())), preferred_element_type=f32
        )
    values = jnp.concatenate([values, jnp.zeros((OWN, 128 - RPAD), f32)], axis=1)
    values = jnp.concatenate([values, jnp.zeros((OPAD - OWN, 128), f32)], axis=0).T
    best = None
    for a in range(ACTS):
        acted = sum(values[(p * ACTS + a) * NF : (p * ACTS + a + 1) * NF] for p in range(PARTS))
        best = acted if best is None else jnp.maximum(best, acted)
    flop_id = lax.broadcasted_iota(jnp.int32, (NF, OPAD), 0)
    scale = jnp.zeros((NF, OPAD), f32)
    weight = jnp.float32(0)
    for f in range(NF):
        iso = iso_smem[f].astype(f32)
        weight += iso
        scale = jnp.where(flop_id == f, iso / live_smem[f].astype(f32), scale)
    partial = jnp.sum(best * scale, axis=0, keepdims=True)
    partial = jnp.where(lax.broadcasted_iota(jnp.int32, (1, OPAD), 1) == OWN, weight, partial)
    final[pl.ds(board, 1)] = partial[None]
    ours = final.at[pl.ds(board, 1)]
    fifth = [
        remote(ours, ours, s5.at[k - 1], r5.at[k - 1], (board + k) % NB, hand) for k in range(1, NB)
    ]
    for c in fifth:
        c.start()
    for c in fifth:
        c.wait_recv()
    whole = jnp.sum(final[...], axis=0)
    out_ref[...] = whole[:, 0:OWN] / whole[:, OWN : OWN + 1]
    for c in first + second + third + fourth + fifth:
        c.wait_send()


def body(reach_pre, strategy, ranks, boards, river_live, iso_weight, pot, line_act):
    anywhere = pl.BlockSpec(memory_space=pl.ANY)
    smem = pl.BlockSpec(memory_space=pltpu.SMEM)
    dma = pltpu.SemaphoreType.DMA
    out = pl.pallas_call(
        kernel,
        out_shape=jax.ShapeDtypeStruct((1, OWN), f32),
        in_specs=[anywhere] * 7 + [smem] * 2,
        out_specs=pl.BlockSpec(memory_space=pltpu.VMEM),
        scratch_shapes=[
            pltpu.VMEM((CHUNK,), f32),
            pltpu.VMEM((NF, LINES, OWN), bf16),
            pltpu.VMEM((NF, RIV, HPAD), jnp.int32),
            pltpu.VMEM((NF, RIV, 5), jnp.int32),
            pltpu.VMEM((LINES,), f32),
            pltpu.VMEM((LINES,), jnp.int32),
            pltpu.VMEM((8, HPAD), f32),
            pltpu.VMEM((80, HPAD), f32),
            pltpu.VMEM((74, 16, HPAD), bf16),
            pltpu.VMEM((74, OWN, 128), bf16),
            pltpu.VMEM((8, 128), f32),
            pltpu.VMEM((OWN, HPAD), bf16),
            pltpu.VMEM((OWN, NF * HPAD), bf16),
            pltpu.VMEM((RPAD, NF * LINES), bf16),
            pltpu.VMEM((8, 128), f32),
            pltpu.VMEM((ZS, 24, OPAD), f32),
            pltpu.VMEM((24, HPAD), f32),
            pltpu.VMEM((8, 128), f32),
            pltpu.VMEM((128, 1, 128), f32),
            pltpu.VMEM((NB, 1, OPAD), f32),
            dma((7,)), dma((7,)), dma((7,)), dma((3,)), dma((3,)), dma((3,)), dma((3,)),
            dma((3,)), dma((3,)), dma((NB - 1,)), dma((NB - 1,)),
        ],
        compiler_params=pltpu.CompilerParams(collective_id=0, has_side_effects=True, vmem_limit_bytes=60 << 20),
    )(reach_pre, strategy, ranks, boards, pot, line_act, jnp.asarray(card_rows()), river_live, iso_weight)
    return out.reshape(OWN)


def solution(mesh):
    in_specs = (
        P(("board", "hand")),
        P("board", None, "hand"),
        P("board", None, None),
        P("board", None, None),
        P("board"),
        P("board"),
        P(),
        P(),
    )
    return jax.shard_map(body, mesh=mesh, in_specs=in_specs, out_specs=P("hand"), check_vma=False)
```

```python
import functools

import jax
import jax.numpy as jnp
import numpy as np
from jax import lax
from jax.experimental import pallas as pl
from jax.experimental.pallas import tpu as pltpu
from jax.sharding import PartitionSpec as P

HANDS = 1326
HPAD = 1408
RIV = 8
LINES = 128
ACTS = 3
NF = 8
OWN = 352
OPAD = 384
CHUNK = 11
DEAD = 128.0
ZS, NB = 4, 32
PARTS = 3
ROWS = PARTS * ACTS * NF
RPAD = 80
WIDE = 256
SPLIT = (3, 5)
f32, bf16 = jnp.float32, jnp.bfloat16


def card_rows():
    first, second = np.triu_indices(52, 1)
    padding = HPAD - HANDS
    rows = np.zeros((8, HPAD), np.float32)
    rows[0] = np.concatenate([first, np.full(padding, 52)])
    rows[1] = np.concatenate([second, np.full(padding, 53)])
    rows[2] = np.arange(HPAD) < HANDS
    return rows


def pieces(value):
    high = value.astype(bf16)
    rest = value - high.astype(f32)
    middle = rest.astype(bf16)
    low = (rest - middle.astype(f32)).astype(bf16)
    return high, middle, low


def kernel(
    reach_hbm, strategy_hbm, ranks_hbm, boards_hbm, pot_hbm, act_hbm, cards_hbm, live_hbm, iso_hbm,
    out_ref,
    reach_in, strat, ranks, boards, pot, act, cards, live_smem, iso_smem,
    rk, rows_b, cols_b, block, mat, sel, spots, wslot, wall, gathered, final,
    load_sem, s1, r1, s2, r2, s4, r4, s5, r5,
):
    board, hand = lax.axis_index("board"), lax.axis_index("hand")

    reach_load = pltpu.make_async_copy(reach_hbm, reach_in, load_sem.at[0])
    reach_load.start()
    barrier = pltpu.get_barrier_semaphore()

    def greet(b, h):
        pl.semaphore_signal(barrier, inc=1, device_id=(b, h), device_id_type=pl.DeviceIdType.MESH)

    for k in range(1, NB):
        greet((board + k) % NB, hand)
    for k in range(1, ZS):
        greet(board, (hand + k) % ZS)

    loads = [
        pltpu.make_async_copy(a, b, load_sem.at[i + 1])
        for i, (a, b) in enumerate(
            [(cards_hbm, cards), (boards_hbm, boards), (live_hbm, live_smem), (iso_hbm, iso_smem),
             (ranks_hbm, ranks), (pot_hbm, pot), (act_hbm, act), (strategy_hbm, strat)]
        )
    ]
    for c in loads:
        c.start()
    reach_load.wait()
    gathered[pl.ds(hand, 1), pl.ds(board, 1), 0:1, 0:CHUNK] = reach_in[...].reshape(1, 1, 1, CHUNK)

    def remote(src, dst, send, recv, b, h):
        return pltpu.make_async_remote_copy(
            src_ref=src, dst_ref=dst, send_sem=send, recv_sem=recv,
            device_id=(b, h), device_id_type=pl.DeviceIdType.MESH,
        )

    pl.semaphore_wait(barrier, NB - 1 + ZS - 1)
    row = gathered.at[hand, pl.ds(board, 1)]
    first = [
        remote(row, row, s1.at[k - 1], r1.at[k - 1], (board + k) % NB, hand) for k in range(1, NB)
    ]
    for c in first:
        c.start()
    for c in loads[:5]:
        c.wait()

    c1, c2, alive = cards[0:1, :], cards[1:2, :], cards[2:3, :]
    runout = lax.broadcasted_iota(jnp.int32, (RIV, 1), 0)
    for f in range(NF):
        dead = jnp.broadcast_to(alive < 0.5, (RIV, HPAD))
        for k in range(5):
            card = boards[k, f].astype(f32).reshape(1, RIV)
            card = jnp.broadcast_to(card, (RIV, RIV))
            diagonal = lax.broadcasted_iota(jnp.int32, (RIV, RIV), 0) == lax.broadcasted_iota(jnp.int32, (RIV, RIV), 1)
            card = jnp.sum(jnp.where(diagonal, card, 0.0), axis=1, keepdims=True)
            dead = dead | (c1 == card) | (c2 == card)
        dead = dead | (runout >= live_smem[f])
        here = jnp.where(dead, DEAD, ranks[f].astype(f32))
        rk[RIV * f : RIV * (f + 1), :] = here
        rk[64 + f : 65 + f, :] = jnp.sum(dead.astype(f32), axis=0, keepdims=True)
    rk[72:74, :] = cards[0:2, :]
    rk[74:80, :] = jnp.zeros((6, HPAD), f32)

    own = rk[:, 0:OPAD]
    for z in range(1, ZS):
        if z < ZS - 1:
            part = rk[:, OWN * z : OWN * z + OPAD]
        else:
            part = jnp.concatenate([rk[:, OWN * z :], jnp.zeros((80, OPAD - OWN), f32)], axis=1)
        own = jnp.where(hand == z, part, own)
    own = jnp.concatenate([own, jnp.zeros((48, OPAD), f32)], axis=0)
    columns = own.T[0:OWN, :]
    for q in range(74):
        cols_b[q] = jnp.broadcast_to(columns[:, q : q + 1], (OWN, WIDE)).astype(bf16)
    for q in range(74):
        rows_b[q] = jnp.broadcast_to(rk[q : q + 1, :], (8, HPAD)).astype(bf16)

    one = jnp.ones((), bf16)

    def spread(row):
        return jnp.broadcast_to(row[None], (OWN // 8, 8, row.shape[1])).reshape(OWN, row.shape[1])

    def block_of(at, wide):
        a1, a2 = cols_b[72, :, 0:wide], cols_b[73, :, 0:wide]
        b1, b2 = spread(rows_b[72, :, at]), spread(rows_b[73, :, at])
        product = ((a1 - b1) * (a1 - b2)) * ((a2 - b1) * (a2 - b2))
        block[:, at] = jnp.minimum(jnp.abs(product), one)

    def tile_of_block(t, carry):
        block_of(pl.ds(pl.multiple_of(t * WIDE, WIDE), WIDE), WIDE)
        return carry

    lax.fori_loop(0, HPAD // WIDE, tile_of_block, 0)
    block_of(pl.ds(HPAD // WIDE * WIDE, 128), 128)

    def build_at(f, start, wide):
        at = pl.ds(start, wide)
        acc = spread(rows_b[64 + f, :, at]) - cols_b[64 + f, :, 0:wide]
        for r in range(RIV):
            gap = cols_b[RIV * f + r, :, 0:wide] - spread(rows_b[RIV * f + r, :, at])
            acc = acc + jnp.maximum(jnp.minimum(gap, one), -one)
        mat[:, pl.ds(pl.multiple_of(f * HPAD + start, 128), wide)] = acc * block[:, at]

    def build(lo, hi):
        tiles = HPAD // WIDE

        def step(i, carry):
            build_at(i // tiles, pl.multiple_of((i % tiles) * WIDE, WIDE), WIDE)
            return carry

        def tail(f, carry):
            build_at(f, tiles * WIDE, 128)
            return carry

        lax.fori_loop(lo * tiles, hi * tiles, step, 0)
        lax.fori_loop(lo, hi, tail, 0)

    for c in loads[5:7]:
        c.wait()
    flop_of_row = lax.broadcasted_iota(jnp.int32, (NF, 128), 0)
    pot_row, act_row = pot[...].reshape(1, LINES), act[...].reshape(1, LINES)
    weights = [pieces(jnp.where(act_row == a, pot_row, 0.0)) for a in range(ACTS)]
    for f in range(NF):
        groups = [
            jnp.where(flop_of_row == f, jnp.broadcast_to(weights[a][p].astype(f32), (NF, LINES)), 0.0)
            for p in range(PARTS) for a in range(ACTS)
        ] + [jnp.zeros((NF, LINES), f32)]
        sel[f] = jnp.concatenate(groups, axis=0).astype(bf16)

    at_hand = lax.broadcasted_iota(jnp.int32, (OWN, 128), 0)
    at_lane = lax.broadcasted_iota(jnp.int32, (OWN, 128), 1)
    chunk = at_hand // CHUNK
    place = (chunk % ZS) * 8 + chunk // ZS
    spots[...] = ((at_lane % 32 == place) & (at_lane < 96)).astype(f32).astype(bf16)

    build(0, SPLIT[0])
    for c in first:
        c.wait_recv()
    plane = gathered.at[pl.ds(hand, 1)]
    second = [
        remote(plane, plane, s2.at[k - 1], r2.at[k - 1], board, (hand + k) % ZS) for k in (2, 1, 3)
    ]
    for c in second:
        c.start()
    build(SPLIT[0], SPLIT[1])
    loads[7].wait()
    for c in second:
        c.wait_recv()

    every = gathered[:, :, 0, :].reshape(128, 128)
    at_row = lax.broadcasted_iota(jnp.int32, (128, 128), 0)
    lane = lax.broadcasted_iota(jnp.int32, (128, 128), 1)
    entry = ((at_row % 32) * ZS + at_row // 32) * CHUNK + lane
    total = jnp.sum(jnp.where((lane < CHUNK) & (entry < HANDS), every, 0.0))
    quarter = jnp.concatenate([gathered[z, pl.ds(hand * 8, 8), 0, :] for z in range(ZS)], axis=0)
    stacked = jnp.concatenate([p.astype(f32) for p in pieces(quarter / total)] + [jnp.zeros((32, 128), f32)], axis=0)
    laid = jnp.dot(spots[...], stacked.astype(bf16), preferred_element_type=f32)
    share = jnp.sum(jnp.where(at_lane == at_hand - chunk * CHUNK, laid, 0.0), axis=1, keepdims=True)

    summed = jnp.zeros((RPAD, OWN), f32)
    for f in range(NF):
        lines = (strat[f].astype(f32) * share).astype(bf16)
        summed += lax.dot_general(sel[f], lines, (((1,), (1,)), ((), ())), preferred_element_type=f32)
    wslot[pl.ds(hand, 1), :, 0:OWN] = (summed[0:24] + summed[24:48] + summed[48:72])[None]
    held = wslot.at[pl.ds(hand, 1)]
    fourth = [
        remote(held, held, s4.at[k - 1], r4.at[k - 1], board, (hand + k) % ZS) for k in (2, 1, 3)
    ]
    for c in fourth:
        c.start()
    build(SPLIT[1], NF)
    for c in fourth:
        c.wait_recv()

    for z in range(ZS):
        wall[:, OWN * z : OWN * (z + 1)] = wslot[z, :, 0:OWN]
    cut = [p.astype(f32) for p in pieces(wall[...])]
    flop_of_lane = lax.broadcasted_iota(jnp.int32, (NF, HPAD), 0)
    values = jnp.zeros((OWN, RPAD), f32)
    for f in range(NF):
        groups = [
            jnp.where(flop_of_lane == f, cut[p][NF * a : NF * (a + 1)], 0.0)
            for p in range(PARTS) for a in range(ACTS)
        ] + [jnp.zeros((NF, HPAD), f32)]
        right = jnp.concatenate(groups, axis=0).astype(bf16)
        values += lax.dot_general(
            mat[:, HPAD * f : HPAD * (f + 1)], right, (((1,), (1,)), ((), ())), preferred_element_type=f32
        )
    values = jnp.concatenate([values, jnp.zeros((OWN, 128 - RPAD), f32)], axis=1)
    values = jnp.concatenate([values, jnp.zeros((OPAD - OWN, 128), f32)], axis=0).T
    best = None
    for a in range(ACTS):
        acted = sum(values[(p * ACTS + a) * NF : (p * ACTS + a + 1) * NF] for p in range(PARTS))
        best = acted if best is None else jnp.maximum(best, acted)
    flop_id = lax.broadcasted_iota(jnp.int32, (NF, OPAD), 0)
    scale = jnp.zeros((NF, OPAD), f32)
    weight = jnp.float32(0)
    for f in range(NF):
        iso = iso_smem[f].astype(f32)
        weight += iso
        scale = jnp.where(flop_id == f, iso / live_smem[f].astype(f32), scale)
    partial = jnp.sum(best * scale, axis=0, keepdims=True)
    partial = jnp.where(lax.broadcasted_iota(jnp.int32, (1, OPAD), 1) == OWN, weight, partial)
    final[pl.ds(board, 1)] = partial[None]
    ours = final.at[pl.ds(board, 1)]
    fifth = [
        remote(ours, ours, s5.at[k - 1], r5.at[k - 1], (board + k) % NB, hand) for k in range(1, NB)
    ]
    for c in fifth:
        c.start()
    for c in fifth:
        c.wait_recv()
    whole = jnp.sum(final[...], axis=0)
    out_ref[...] = (whole[:, 0:OWN] / whole[:, OWN : OWN + 1]).reshape(OWN)
    for c in first + second + fourth + fifth:
        c.wait_send()


def body(reach_pre, strategy, ranks, boards, river_live, iso_weight, pot, line_act):
    anywhere = pl.BlockSpec(memory_space=pl.ANY)
    dma = pltpu.SemaphoreType.DMA
    return pl.pallas_call(
        kernel,
        out_shape=jax.ShapeDtypeStruct((OWN,), f32),
        in_specs=[anywhere] * 9,
        out_specs=pl.BlockSpec(memory_space=pltpu.VMEM),
        scratch_shapes=[
            pltpu.VMEM((CHUNK,), f32),
            pltpu.VMEM((NF, OWN, LINES), bf16),
            pltpu.VMEM((NF, RIV, HPAD), jnp.int32),
            pltpu.VMEM((5, NF, RIV), jnp.int32),
            pltpu.VMEM((LINES,), f32),
            pltpu.VMEM((LINES,), jnp.int32),
            pltpu.VMEM((8, HPAD), f32),
            pltpu.SMEM((NF,), jnp.int32),
            pltpu.SMEM((NF,), jnp.int32),
            pltpu.VMEM((80, HPAD), f32),
            pltpu.VMEM((74, 8, HPAD), bf16),
            pltpu.VMEM((74, OWN, WIDE), bf16),
            pltpu.VMEM((OWN, HPAD), bf16),
            pltpu.VMEM((OWN, NF * HPAD), bf16),
            pltpu.VMEM((NF, RPAD, LINES), bf16),
            pltpu.VMEM((OWN, 128), bf16),
            pltpu.VMEM((ZS, 24, OPAD), f32),
            pltpu.VMEM((24, HPAD), f32),
            pltpu.VMEM((ZS, NB, 1, 128), f32),
            pltpu.VMEM((NB, 1, OPAD), f32),
            dma((9,)), dma((NB - 1,)), dma((NB - 1,)), dma((3,)), dma((3,)), dma((3,)), dma((3,)),
            dma((NB - 1,)), dma((NB - 1,)),
        ],
        compiler_params=pltpu.CompilerParams(collective_id=0, has_side_effects=True, vmem_limit_bytes=60 << 20),
    )(
        reach_pre, jnp.swapaxes(strategy, 1, 2), ranks, jnp.transpose(boards, (2, 0, 1)),
        pot, line_act, jnp.asarray(card_rows()), river_live, iso_weight,
    )


def solution(mesh):
    in_specs = (
        P(("board", "hand")),
        P("board", None, "hand"),
        P("board", None, None),
        P("board", None, None),
        P("board"),
        P("board"),
        P(),
        P(),
    )
    return jax.shard_map(body, mesh=mesh, in_specs=in_specs, out_specs=P("hand"), check_vma=False)
```

```python
import functools

import jax
import jax.numpy as jnp
import numpy as np
from jax import lax
from jax.experimental import pallas as pl
from jax.experimental.pallas import tpu as pltpu
from jax.sharding import PartitionSpec as P

HANDS = 1326
HPAD = 1408
RIV = 8
LINES = 128
ACTS = 3
NF = 8
OWN = 352
OPAD = 384
CHUNK = 11
DEAD = 128.0
ZS, NB = 4, 32
PARTS = 3
ROWS = PARTS * ACTS * NF
RPAD = 80
HALF = NF // 2
KPAD = ZS * OPAD
STEP = 128
TOP = 96
SPLIT = (3, 6)
f32, bf16, f8 = jnp.float32, jnp.bfloat16, jnp.float8_e4m3fn


def card_rows():
    first, second = np.triu_indices(52, 1)
    padding = HPAD - HANDS
    rows = np.zeros((ZS, 8, OPAD), np.float32)
    rows[:, 0], rows[:, 1] = 52, 53
    rows[:, 0, :OWN] = np.concatenate([first, np.full(padding, 52)]).reshape(ZS, OWN)
    rows[:, 1, :OWN] = np.concatenate([second, np.full(padding, 53)]).reshape(ZS, OWN)
    rows[:, 2, :OWN] = (np.arange(HPAD) < HANDS).reshape(ZS, OWN)
    return rows


def pieces(value):
    high = value.astype(bf16)
    rest = value - high.astype(f32)
    middle = rest.astype(bf16)
    low = (rest - middle.astype(f32)).astype(bf16)
    return high, middle, low


def kernel(
    reach_hbm, strategy_hbm, ranks_hbm, boards_hbm, pot_hbm, act_hbm, cards_hbm, live_hbm, iso_hbm,
    out_ref,
    reach_in, strat, ranks, boards, pot, act, cards, live_smem, iso_smem,
    quarters, rel, inc, lhs, slots, onehot, block, mat, sel, spots, scales, wslot, sums, gathered, final,
    load_sem, s1, r1, s2, r2, s4, r4, s5, r5,
):
    board, hand = lax.axis_index("board"), lax.axis_index("hand")
    plane_ids = [(board + k) % NB for k in range(1, NB)]

    reach_load = pltpu.make_async_copy(reach_hbm, reach_in, load_sem.at[0])
    reach_load.start()
    barrier = pltpu.get_barrier_semaphore()

    def greet(b, h):
        pl.semaphore_signal(barrier, inc=1, device_id=(b, h), device_id_type=pl.DeviceIdType.MESH)

    for b in plane_ids:
        greet(b, hand)
    for k in (2, 1, 3):
        greet(board, (hand + k) % ZS)

    loads = [
        pltpu.make_async_copy(a, b, load_sem.at[i + 1])
        for i, (a, b) in enumerate(
            [(cards_hbm, cards), (boards_hbm, boards), (live_hbm, live_smem), (iso_hbm, iso_smem),
             (ranks_hbm, ranks), (pot_hbm, pot), (act_hbm, act), (strategy_hbm, strat)]
        )
    ]
    for c in loads:
        c.start()
    reach_load.wait()
    gathered[pl.ds(hand, 1), pl.ds(board, 1), 0:1, 0:CHUNK] = reach_in[...].reshape(1, 1, 1, CHUNK)

    def remote(src, dst, send, recv, b, h):
        return pltpu.make_async_remote_copy(
            src_ref=src, dst_ref=dst, send_sem=send, recv_sem=recv,
            device_id=(b, h), device_id_type=pl.DeviceIdType.MESH,
        )

    pl.semaphore_wait(barrier, NB - 1 + ZS - 1)
    row = gathered.at[hand, pl.ds(board, 1)]
    first = [remote(row, row, s1.at[i], r1.at[i], b, hand) for i, b in enumerate(plane_ids)]
    for c in first:
        c.start()
    for c in loads[:5]:
        c.wait()

    runout = lax.broadcasted_iota(jnp.int32, (RIV, 1), 0)
    diagonal = lax.broadcasted_iota(jnp.int32, (RIV, RIV), 0) == lax.broadcasted_iota(jnp.int32, (RIV, RIV), 1)
    for f in range(NF):
        drawn = []
        for k in range(5):
            card = jnp.broadcast_to(boards[k, f].astype(f32).reshape(1, RIV), (RIV, RIV))
            drawn.append(jnp.sum(jnp.where(diagonal, card, 0.0), axis=1, keepdims=True))
        beyond = runout >= live_smem[f]
        for z in range(ZS):
            if z < ZS - 1:
                part = ranks[f, :, OWN * z : OWN * z + OPAD].astype(f32)
            else:
                part = jnp.concatenate([ranks[f, :, OWN * z :].astype(f32), jnp.zeros((RIV, OPAD - OWN), f32)], axis=1)
            dead = (cards[z, 2:3, :] < 0.5) | beyond
            for card in drawn:
                dead = dead | (cards[z, 0:1, :] == card) | (cards[z, 1:2, :] == card)
            quarters[z, RIV * f : RIV * (f + 1), :] = jnp.where(dead, DEAD, part)
    card_id = lax.broadcasted_iota(jnp.int32, (128, OPAD), 0).astype(f32)
    for z in range(ZS):
        inc[z] = ((card_id == cards[z, 0:1, :]) | (card_id == cards[z, 1:2, :])).astype(f32)

    for k in range(ZS):
        rel[:, OPAD * k : OPAD * (k + 1)] = quarters[(hand + ZS - k) % ZS]
    own = quarters[hand]
    alive = (own < DEAD).astype(f32)
    ranked = own * alive
    both = [t for f in range(NF) for t in (ranked[RIV * f : RIV * (f + 1)], alive[RIV * f : RIV * (f + 1)])]
    lhs[...] = jnp.concatenate(both, axis=0).T[0:OWN].astype(bf16)
    held_cards = inc[hand].T[0:OWN].astype(bf16)
    for k in range(ZS):
        shared = jnp.dot(held_cards, inc[(hand + ZS - k) % ZS].astype(bf16), preferred_element_type=f32)
        block[:, OPAD * k : OPAD * (k + 1)] = jnp.where(shared > 0.5, 0.0, 1.0).astype(bf16)

    slots[...] = jnp.zeros(slots.shape, bf16)
    at = lax.broadcasted_iota(jnp.int32, (2 * RIV, RIV * STEP), 1)
    which = lax.broadcasted_iota(jnp.int32, (2 * RIV, RIV * STEP), 0)
    pattern = jnp.where(which < RIV, 1.0, -(at % STEP).astype(f32))
    slots[112:128, :] = jnp.where(at // STEP == which % RIV, pattern, 0.0).astype(bf16)
    for r in range(RIV):
        onehot[STEP * r + TOP : STEP * (r + 1), :] = jnp.zeros((STEP - TOP, KPAD), bf16).astype(f8)
    slot = lax.broadcasted_iota(jnp.int32, (TOP, KPAD), 0).astype(f32).astype(bf16)
    one, zero = jnp.ones((), bf16), jnp.zeros((), bf16)

    def build(lo, hi):
        def step(f, carry):
            pick = slots[pl.ds(pl.multiple_of(112 - 16 * f, 16), 128), :]
            beats = jnp.dot(lhs[...], pick, preferred_element_type=f32)
            beats = jnp.maximum(jnp.minimum(beats, 1.0), -1.0).astype(bf16).astype(f8)
            for r in range(RIV):
                ranked = jnp.broadcast_to(rel[pl.ds(RIV * f + r, 1), :], (TOP, KPAD)).astype(bf16)
                onehot[STEP * r : STEP * r + TOP, :] = jnp.where(slot == ranked, one, zero).astype(f8)
            net = jnp.dot(beats, onehot[...], preferred_element_type=f32)
            for k in range(ZS):
                here = net[:, OPAD * k : OPAD * (k + 1)].astype(bf16) * block[:, OPAD * k : OPAD * (k + 1)]
                start = ((f // HALF) * ZS + k) * HALF * OPAD + (f % HALF) * OPAD
                mat[:, pl.ds(pl.multiple_of(start, 128), OPAD)] = here
            return carry

        lax.fori_loop(lo, hi, step, 0)

    for c in loads[5:7]:
        c.wait()
    lines_row = lax.broadcasted_iota(jnp.int32, (HALF, LINES), 0)
    pot_row, act_row = pot[...].reshape(1, LINES), act[...].reshape(1, LINES)
    weights = [pieces(jnp.where(act_row == a, pot_row, 0.0)) for a in range(ACTS)]
    for f in range(HALF):
        groups = [
            jnp.where(lines_row == f, jnp.broadcast_to(weights[a][p].astype(f32), (HALF, LINES)), 0.0)
            for p in range(PARTS) for a in range(ACTS)
        ] + [jnp.zeros((HALF, LINES), f32)]
        sel[f] = jnp.concatenate(groups, axis=0).astype(bf16)

    flop_id = lax.broadcasted_iota(jnp.int32, (NF, OPAD), 0)
    scale = jnp.zeros((NF, OPAD), f32)
    weight = jnp.float32(0)
    for f in range(NF):
        iso = iso_smem[f].astype(f32)
        weight += iso
        scale = jnp.where(flop_id == f, iso / live_smem[f].astype(f32), scale)
    scales[0] = scale
    scales[1] = jnp.full((NF, OPAD), weight)

    at_hand = lax.broadcasted_iota(jnp.int32, (OWN, 128), 0)
    at_lane = lax.broadcasted_iota(jnp.int32, (OWN, 128), 1)
    chunk = at_hand // CHUNK
    place = (chunk % ZS) * 8 + chunk // ZS
    spots[...] = ((at_lane % 32 == place) & (at_lane < 96)).astype(f32).astype(bf16)

    build(0, SPLIT[0])
    for c in first:
        c.wait_recv()
    plane = gathered.at[pl.ds(hand, 1)]
    second = [
        remote(plane, plane, s2.at[k - 1], r2.at[k - 1], board, (hand + k) % ZS) for k in (2, 1, 3)
    ]
    for c in second:
        c.start()
    build(SPLIT[0], SPLIT[1])
    loads[7].wait()
    for c in second:
        c.wait_recv()

    every = gathered[:, :, 0, :].reshape(128, 128)
    at_row = lax.broadcasted_iota(jnp.int32, (128, 128), 0)
    lane = lax.broadcasted_iota(jnp.int32, (128, 128), 1)
    entry = ((at_row % 32) * ZS + at_row // 32) * CHUNK + lane
    total = jnp.sum(jnp.where((lane < CHUNK) & (entry < HANDS), every, 0.0))
    quarter = jnp.concatenate([gathered[z, pl.ds(hand * 8, 8), 0, :] for z in range(ZS)], axis=0)
    stacked = jnp.concatenate([p.astype(f32) for p in pieces(quarter / total)] + [jnp.zeros((32, 128), f32)], axis=0)
    laid = jnp.dot(spots[...], stacked.astype(bf16), preferred_element_type=f32)
    share = jnp.sum(jnp.where(at_lane == at_hand - chunk * CHUNK, laid, 0.0), axis=1, keepdims=True)

    sent = []
    for h in range(2):
        summed = jnp.zeros((40, OWN), f32)
        for f in range(HALF):
            lines = (strat[HALF * h + f].astype(f32) * share).astype(bf16)
            summed += lax.dot_general(sel[f], lines, (((1,), (1,)), ((), ())), preferred_element_type=f32)
        summed = jnp.concatenate([summed, jnp.zeros((40, OPAD - OWN), f32)], axis=1)
        wslot[pl.ds(hand, 1), h] = (summed[0:12] + summed[12:24] + summed[24:36])[None]
        held = wslot.at[pl.ds(hand, 1), h]
        sent.append([
            remote(held, held, s4.at[3 * h + k - 1], r4.at[3 * h + k - 1], board, (hand + k) % ZS) for k in (2, 1, 3)
        ])
        for c in sent[h]:
            c.start()
    build(SPLIT[1], NF)

    flop_of_lane = lax.broadcasted_iota(jnp.int32, (NF, OPAD), 0)

    def times_reach(h, k):
        cut = [p.astype(f32) for p in pieces(wslot[(hand + ZS - k) % ZS, h])]
        columns = []
        for f in range(HALF):
            groups = [
                jnp.where(flop_of_lane == HALF * h + f, cut[p][HALF * a + f : HALF * a + f + 1], 0.0)
                for p in range(PARTS) for a in range(ACTS)
            ] + [jnp.zeros((NF, OPAD), f32)]
            columns.append(jnp.concatenate(groups, axis=0).astype(bf16))
        return columns

    def product(h, ks):
        right = jnp.concatenate([c for k in ks for c in times_reach(h, k)], axis=1)
        start = (h * ZS + ks[0]) * HALF * OPAD
        left = mat[:, start : start + len(ks) * HALF * OPAD]
        return lax.dot_general(left, right, (((1,), (1,)), ((), ())), preferred_element_type=f32)

    sums[...] = product(0, (0,)) + product(1, (0,))
    for h in range(2):
        for c in sent[h]:
            c.wait_recv()
        sums[...] += product(h, (1, 2)) + product(h, (3,))
    values = sums[...]
    values = jnp.concatenate([values, jnp.zeros((OWN, 128 - RPAD), f32)], axis=1)
    values = jnp.concatenate([values, jnp.zeros((OPAD - OWN, 128), f32)], axis=0).T
    best = None
    for a in range(ACTS):
        acted = sum(values[(p * ACTS + a) * NF : (p * ACTS + a + 1) * NF] for p in range(PARTS))
        best = acted if best is None else jnp.maximum(best, acted)
    partial = jnp.sum(best * scales[0], axis=0, keepdims=True)
    partial = jnp.where(lax.broadcasted_iota(jnp.int32, (1, OPAD), 1) == OWN, scales[1, 0:1], partial)
    final[pl.ds(board, 1)] = partial[None]
    ours = final.at[pl.ds(board, 1)]
    fifth = [remote(ours, ours, s5.at[i], r5.at[i], b, hand) for i, b in enumerate(plane_ids)]
    for c in fifth:
        c.start()
    for c in fifth:
        c.wait_recv()
    whole = jnp.sum(final[...], axis=0)
    out_ref[...] = (whole[:, 0:OWN] / whole[:, OWN : OWN + 1]).reshape(OWN)
    for c in first + second + sent[0] + sent[1] + fifth:
        c.wait_send()


def body(reach_pre, strategy, ranks, boards, river_live, iso_weight, pot, line_act):
    anywhere = pl.BlockSpec(memory_space=pl.ANY)
    dma = pltpu.SemaphoreType.DMA
    return pl.pallas_call(
        kernel,
        out_shape=jax.ShapeDtypeStruct((OWN,), f32),
        in_specs=[anywhere] * 9,
        out_specs=pl.BlockSpec(memory_space=pltpu.VMEM),
        scratch_shapes=[
            pltpu.VMEM((CHUNK,), f32),
            pltpu.VMEM((NF, OWN, LINES), bf16),
            pltpu.VMEM((NF, RIV, HPAD), jnp.int32),
            pltpu.VMEM((5, NF, RIV), jnp.int32),
            pltpu.VMEM((LINES,), f32),
            pltpu.VMEM((LINES,), jnp.int32),
            pltpu.VMEM((ZS, 8, OPAD), f32),
            pltpu.SMEM((NF,), jnp.int32),
            pltpu.SMEM((NF,), jnp.int32),
            pltpu.VMEM((ZS, NF * RIV, OPAD), f32),
            pltpu.VMEM((NF * RIV, KPAD), f32),
            pltpu.VMEM((ZS, 128, OPAD), f32),
            pltpu.VMEM((OWN, 128), bf16),
            pltpu.VMEM((256, RIV * STEP), bf16),
            pltpu.VMEM((RIV * STEP, KPAD), f8),
            pltpu.VMEM((OWN, KPAD), bf16),
            pltpu.VMEM((OWN, NF * KPAD), bf16),
            pltpu.VMEM((HALF, 40, LINES), bf16),
            pltpu.VMEM((OWN, 128), bf16),
            pltpu.VMEM((2, NF, OPAD), f32),
            pltpu.VMEM((ZS, 2, ACTS * HALF, OPAD), f32),
            pltpu.VMEM((OWN, RPAD), f32),
            pltpu.VMEM((ZS, NB, 1, 128), f32),
            pltpu.VMEM((NB, 1, OPAD), f32),
            dma((9,)), dma((NB - 1,)), dma((NB - 1,)), dma((3,)), dma((3,)), dma((6,)), dma((6,)),
            dma((NB - 1,)), dma((NB - 1,)),
        ],
        compiler_params=pltpu.CompilerParams(collective_id=0, has_side_effects=True, vmem_limit_bytes=60 << 20),
    )(
        reach_pre, jnp.swapaxes(strategy, 1, 2), ranks, jnp.transpose(boards, (2, 0, 1)),
        pot, line_act, jnp.asarray(card_rows()), river_live, iso_weight,
    )


def solution(mesh):
    in_specs = (
        P(("board", "hand")),
        P("board", None, "hand"),
        P("board", None, None),
        P("board", None, None),
        P("board"),
        P("board"),
        P(),
        P(),
    )
    return jax.shard_map(body, mesh=mesh, in_specs=in_specs, out_specs=P("hand"), check_vma=False)
```

```python
import functools

import jax
import jax.numpy as jnp
import numpy as np
from jax import lax
from jax.experimental import pallas as pl
from jax.experimental.pallas import tpu as pltpu
from jax.sharding import PartitionSpec as P

HANDS = 1326
HPAD = 1408
RIV = 8
LINES = 128
ACTS = 3
NF = 8
OWN = 352
OPAD = 384
CHUNK = 11
DEAD = 128.0
ZS, NB = 4, 32
PARTS = 3
ROWS = PARTS * ACTS * NF
RPAD = 80
HALF = NF // 2
KPAD = ZS * OPAD
STEP = 128
TOP = 96
SPLIT = (3, 6)
f32, bf16, f8 = jnp.float32, jnp.bfloat16, jnp.float8_e4m3fn


def card_rows():
    first, second = np.triu_indices(52, 1)
    padding = HPAD - HANDS
    rows = np.zeros((ZS, 8, OPAD), np.float32)
    rows[:, 0], rows[:, 1] = 52, 53
    rows[:, 0, :OWN] = np.concatenate([first, np.full(padding, 52)]).reshape(ZS, OWN)
    rows[:, 1, :OWN] = np.concatenate([second, np.full(padding, 53)]).reshape(ZS, OWN)
    rows[:, 2, :OWN] = (np.arange(HPAD) < HANDS).reshape(ZS, OWN)
    return rows


def pieces(value):
    high = value.astype(bf16)
    rest = value - high.astype(f32)
    middle = rest.astype(bf16)
    low = (rest - middle.astype(f32)).astype(bf16)
    return high, middle, low


def kernel(
    reach_hbm, strategy_hbm, ranks_hbm, boards_hbm, pot_hbm, act_hbm, cards_hbm, live_hbm, iso_hbm,
    out_ref,
    reach_in, strat, ranks, boards, pot, act, cards, live_smem, iso_smem,
    quarters, rel, inc, lhs, slots, onehot, block, mat, sel, spots, scales, wslot, sums, gathered, parts, final,
    load_sem, s1, r1, s2, r2, s3, r3, s4, r4, s5, r5,
):
    board, hand = lax.axis_index("board"), lax.axis_index("hand")
    plane_ids = [(board + k) % NB for k in range(1, NB)]

    reach_load = pltpu.make_async_copy(reach_hbm, reach_in, load_sem.at[0])
    reach_load.start()
    barrier = pltpu.get_barrier_semaphore()

    def greet(b, h):
        pl.semaphore_signal(barrier, inc=1, device_id=(b, h), device_id_type=pl.DeviceIdType.MESH)

    for b in plane_ids:
        greet(b, hand)
    for k in (2, 1, 3):
        greet(board, (hand + k) % ZS)

    loads = [
        pltpu.make_async_copy(a, b, load_sem.at[i + 1])
        for i, (a, b) in enumerate(
            [(cards_hbm, cards), (boards_hbm, boards), (live_hbm, live_smem), (iso_hbm, iso_smem),
             (ranks_hbm, ranks), (pot_hbm, pot), (act_hbm, act), (strategy_hbm, strat)]
        )
    ]
    for c in loads:
        c.start()
    reach_load.wait()
    gathered[pl.ds(hand, 1), pl.ds(board, 1), 0:1, 0:CHUNK] = reach_in[...].reshape(1, 1, 1, CHUNK)

    def remote(src, dst, send, recv, b, h):
        return pltpu.make_async_remote_copy(
            src_ref=src, dst_ref=dst, send_sem=send, recv_sem=recv,
            device_id=(b, h), device_id_type=pl.DeviceIdType.MESH,
        )

    pl.semaphore_wait(barrier, NB - 1 + ZS - 1)
    row = gathered.at[hand, pl.ds(board, 1)]
    first = [remote(row, row, s1.at[i], r1.at[i], b, hand) for i, b in enumerate(plane_ids)]
    for c in first:
        c.start()
    for c in loads[:5]:
        c.wait()

    runout = lax.broadcasted_iota(jnp.int32, (RIV, 1), 0)
    diagonal = lax.broadcasted_iota(jnp.int32, (RIV, RIV), 0) == lax.broadcasted_iota(jnp.int32, (RIV, RIV), 1)
    for f in range(NF):
        drawn = []
        for k in range(5):
            card = jnp.broadcast_to(boards[k, f].astype(f32).reshape(1, RIV), (RIV, RIV))
            drawn.append(jnp.sum(jnp.where(diagonal, card, 0.0), axis=1, keepdims=True))
        beyond = runout >= live_smem[f]
        for z in range(ZS):
            if z < ZS - 1:
                part = ranks[f, :, OWN * z : OWN * z + OPAD].astype(f32)
            else:
                part = jnp.concatenate([ranks[f, :, OWN * z :].astype(f32), jnp.zeros((RIV, OPAD - OWN), f32)], axis=1)
            dead = (cards[z, 2:3, :] < 0.5) | beyond
            for card in drawn:
                dead = dead | (cards[z, 0:1, :] == card) | (cards[z, 1:2, :] == card)
            quarters[z, RIV * f : RIV * (f + 1), :] = jnp.where(dead, DEAD, part)
    card_id = lax.broadcasted_iota(jnp.int32, (128, OPAD), 0).astype(f32)
    for z in range(ZS):
        inc[z] = ((card_id == cards[z, 0:1, :]) | (card_id == cards[z, 1:2, :])).astype(f32)

    for k in range(ZS):
        rel[:, OPAD * k : OPAD * (k + 1)] = quarters[(hand + ZS - k) % ZS]
    own = quarters[hand]
    alive = (own < DEAD).astype(f32)
    ranked = own * alive
    both = [t for f in range(NF) for t in (ranked[RIV * f : RIV * (f + 1)], alive[RIV * f : RIV * (f + 1)])]
    lhs[...] = jnp.concatenate(both, axis=0).T[0:OWN].astype(bf16)
    held_cards = inc[hand].T[0:OWN].astype(bf16)
    for k in range(ZS):
        shared = jnp.dot(held_cards, inc[(hand + ZS - k) % ZS].astype(bf16), preferred_element_type=f32)
        block[:, OPAD * k : OPAD * (k + 1)] = jnp.where(shared > 0.5, 0.0, 1.0).astype(bf16)

    slots[...] = jnp.zeros(slots.shape, bf16)
    at = lax.broadcasted_iota(jnp.int32, (2 * RIV, RIV * STEP), 1)
    which = lax.broadcasted_iota(jnp.int32, (2 * RIV, RIV * STEP), 0)
    pattern = jnp.where(which < RIV, 1.0, -(at % STEP).astype(f32))
    slots[112:128, :] = jnp.where(at // STEP == which % RIV, pattern, 0.0).astype(bf16)
    for r in range(RIV):
        onehot[STEP * r + TOP : STEP * (r + 1), :] = jnp.zeros((STEP - TOP, KPAD), bf16).astype(f8)
    slot = lax.broadcasted_iota(jnp.int32, (TOP, KPAD), 0).astype(f32).astype(bf16)
    one, zero = jnp.ones((), bf16), jnp.zeros((), bf16)

    def build(lo, hi):
        def step(f, carry):
            pick = slots[pl.ds(pl.multiple_of(112 - 16 * f, 16), 128), :]
            beats = jnp.dot(lhs[...], pick, preferred_element_type=f32)
            beats = jnp.maximum(jnp.minimum(beats, 1.0), -1.0).astype(bf16).astype(f8)
            for r in range(RIV):
                ranked = jnp.broadcast_to(rel[pl.ds(RIV * f + r, 1), :], (TOP, KPAD)).astype(bf16)
                onehot[STEP * r : STEP * r + TOP, :] = jnp.where(slot == ranked, one, zero).astype(f8)
            net = jnp.dot(beats, onehot[...], preferred_element_type=f32)
            for k in range(ZS):
                here = net[:, OPAD * k : OPAD * (k + 1)].astype(bf16) * block[:, OPAD * k : OPAD * (k + 1)]
                start = ((f // HALF) * ZS + k) * HALF * OPAD + (f % HALF) * OPAD
                mat[:, pl.ds(pl.multiple_of(start, 128), OPAD)] = here
            return carry

        lax.fori_loop(lo, hi, step, 0)

    for c in loads[5:7]:
        c.wait()
    lines_row = lax.broadcasted_iota(jnp.int32, (HALF, LINES), 0)
    pot_row, act_row = pot[...].reshape(1, LINES), act[...].reshape(1, LINES)
    weights = [pieces(jnp.where(act_row == a, pot_row, 0.0)) for a in range(ACTS)]
    for f in range(HALF):
        groups = [
            jnp.where(lines_row == f, jnp.broadcast_to(weights[a][p].astype(f32), (HALF, LINES)), 0.0)
            for p in range(PARTS) for a in range(ACTS)
        ] + [jnp.zeros((HALF, LINES), f32)]
        sel[f] = jnp.concatenate(groups, axis=0).astype(bf16)

    flop_id = lax.broadcasted_iota(jnp.int32, (NF, OPAD), 0)
    scale = jnp.zeros((NF, OPAD), f32)
    weight = jnp.float32(0)
    for f in range(NF):
        iso = iso_smem[f].astype(f32)
        weight += iso
        scale = jnp.where(flop_id == f, iso / live_smem[f].astype(f32), scale)
    scales[0] = scale
    scales[1] = jnp.full((NF, OPAD), weight)

    at_hand = lax.broadcasted_iota(jnp.int32, (OWN, 128), 0)
    at_lane = lax.broadcasted_iota(jnp.int32, (OWN, 128), 1)
    chunk = at_hand // CHUNK
    place = (chunk % ZS) * 8 + chunk // ZS
    spots[...] = ((at_lane % 32 == place) & (at_lane < 96)).astype(f32).astype(bf16)

    build(0, SPLIT[0])
    for c in first:
        c.wait_recv()
    second = []
    for k in (2, 1, 3):
        rows_of = gathered.at[hand, pl.ds(((hand + k) % ZS) * 8, 8)]
        second.append(remote(rows_of, rows_of, s2.at[k - 1], r2.at[k - 1], board, (hand + k) % ZS))
    for c in second:
        c.start()
    plane = gathered[pl.ds(hand, 1), :, 0, :].reshape(NB, 128)
    lane = lax.broadcasted_iota(jnp.int32, (NB, 128), 1)
    entry = (lax.broadcasted_iota(jnp.int32, (NB, 128), 0) * ZS + hand) * CHUNK + lane
    plane = jnp.where((lane < CHUNK) & (entry < HANDS), plane, 0.0)
    parts[pl.ds(hand, 1)] = jnp.sum(plane, axis=0, keepdims=True)[None]
    part = parts.at[pl.ds(hand, 1)]
    third = [remote(part, part, s3.at[k - 1], r3.at[k - 1], board, (hand + k) % ZS) for k in (2, 1, 3)]
    for c in third:
        c.start()
    build(SPLIT[0], SPLIT[1])
    loads[7].wait()
    for c in second + third:
        c.wait_recv()

    total = jnp.sum(jnp.sum(parts[...], axis=0))
    quarter = jnp.concatenate([gathered[z, pl.ds(hand * 8, 8), 0, :] for z in range(ZS)], axis=0)
    stacked = jnp.concatenate([p.astype(f32) for p in pieces(quarter / total)] + [jnp.zeros((32, 128), f32)], axis=0)
    laid = jnp.dot(spots[...], stacked.astype(bf16), preferred_element_type=f32)
    share = jnp.sum(jnp.where(at_lane == at_hand - chunk * CHUNK, laid, 0.0), axis=1, keepdims=True)

    sent = []
    for h in range(2):
        summed = jnp.zeros((40, OWN), f32)
        for f in range(HALF):
            lines = (strat[HALF * h + f].astype(f32) * share).astype(bf16)
            summed += lax.dot_general(sel[f], lines, (((1,), (1,)), ((), ())), preferred_element_type=f32)
        summed = jnp.concatenate([summed, jnp.zeros((40, OPAD - OWN), f32)], axis=1)
        wslot[pl.ds(hand, 1), h] = (summed[0:12] + summed[12:24] + summed[24:36])[None]
        held = wslot.at[pl.ds(hand, 1), h]
        sent.append([
            remote(held, held, s4.at[3 * h + k - 1], r4.at[3 * h + k - 1], board, (hand + k) % ZS) for k in (2, 1, 3)
        ])
        for c in sent[h]:
            c.start()
    build(SPLIT[1], NF)

    flop_of_lane = lax.broadcasted_iota(jnp.int32, (NF, OPAD), 0)

    def times_reach(h, k):
        cut = [p.astype(f32) for p in pieces(wslot[(hand + ZS - k) % ZS, h])]
        columns = []
        for f in range(HALF):
            groups = [
                jnp.where(flop_of_lane == HALF * h + f, cut[p][HALF * a + f : HALF * a + f + 1], 0.0)
                for p in range(PARTS) for a in range(ACTS)
            ] + [jnp.zeros((NF, OPAD), f32)]
            columns.append(jnp.concatenate(groups, axis=0).astype(bf16))
        return columns

    def product(h, ks):
        right = jnp.concatenate([c for k in ks for c in times_reach(h, k)], axis=1)
        start = (h * ZS + ks[0]) * HALF * OPAD
        left = mat[:, start : start + len(ks) * HALF * OPAD]
        return lax.dot_general(left, right, (((1,), (1,)), ((), ())), preferred_element_type=f32)

    sums[...] = jnp.zeros((OWN, RPAD), f32)
    sums[...] += product(0, (0,))
    sums[...] += product(1, (0,))
    for h in range(2):
        for c in sent[h]:
            c.wait_recv()
        sums[...] += product(h, (1, 2, 3))
    values = sums[...]
    values = jnp.concatenate([values, jnp.zeros((OWN, 128 - RPAD), f32)], axis=1)
    values = jnp.concatenate([values, jnp.zeros((OPAD - OWN, 128), f32)], axis=0).T
    best = None
    for a in range(ACTS):
        acted = sum(values[(p * ACTS + a) * NF : (p * ACTS + a + 1) * NF] for p in range(PARTS))
        best = acted if best is None else jnp.maximum(best, acted)
    partial = jnp.sum(best * scales[0], axis=0, keepdims=True)
    partial = jnp.where(lax.broadcasted_iota(jnp.int32, (1, OPAD), 1) == OWN, scales[1, 0:1], partial)
    final[pl.ds(board, 1)] = partial[None]
    ours = final.at[pl.ds(board, 1)]
    fifth = [remote(ours, ours, s5.at[i], r5.at[i], b, hand) for i, b in enumerate(plane_ids)]
    for c in fifth:
        c.start()
    for c in fifth:
        c.wait_recv()
    whole = jnp.sum(final[...], axis=0)
    out_ref[...] = (whole[:, 0:OWN] / whole[:, OWN : OWN + 1]).reshape(OWN)
    for c in first + second + third + sent[0] + sent[1] + fifth:
        c.wait_send()


def body(reach_pre, strategy, ranks, boards, river_live, iso_weight, pot, line_act):
    anywhere = pl.BlockSpec(memory_space=pl.ANY)
    dma = pltpu.SemaphoreType.DMA
    return pl.pallas_call(
        kernel,
        out_shape=jax.ShapeDtypeStruct((OWN,), f32),
        in_specs=[anywhere] * 9,
        out_specs=pl.BlockSpec(memory_space=pltpu.VMEM),
        scratch_shapes=[
            pltpu.VMEM((CHUNK,), f32),
            pltpu.VMEM((NF, OWN, LINES), bf16),
            pltpu.VMEM((NF, RIV, HPAD), jnp.int32),
            pltpu.VMEM((5, NF, RIV), jnp.int32),
            pltpu.VMEM((LINES,), f32),
            pltpu.VMEM((LINES,), jnp.int32),
            pltpu.VMEM((ZS, 8, OPAD), f32),
            pltpu.SMEM((NF,), jnp.int32),
            pltpu.SMEM((NF,), jnp.int32),
            pltpu.VMEM((ZS, NF * RIV, OPAD), f32),
            pltpu.VMEM((NF * RIV, KPAD), f32),
            pltpu.VMEM((ZS, 128, OPAD), f32),
            pltpu.VMEM((OWN, 128), bf16),
            pltpu.VMEM((256, RIV * STEP), bf16),
            pltpu.VMEM((RIV * STEP, KPAD), f8),
            pltpu.VMEM((OWN, KPAD), bf16),
            pltpu.VMEM((OWN, NF * KPAD), bf16),
            pltpu.VMEM((HALF, 40, LINES), bf16),
            pltpu.VMEM((OWN, 128), bf16),
            pltpu.VMEM((2, NF, OPAD), f32),
            pltpu.VMEM((ZS, 2, ACTS * HALF, OPAD), f32),
            pltpu.VMEM((OWN, RPAD), f32),
            pltpu.VMEM((ZS, NB, 1, 128), f32),
            pltpu.VMEM((ZS, 1, 128), f32),
            pltpu.VMEM((NB, 1, OPAD), f32),
            dma((9,)), dma((NB - 1,)), dma((NB - 1,)), dma((3,)), dma((3,)), dma((3,)), dma((3,)), dma((6,)), dma((6,)),
            dma((NB - 1,)), dma((NB - 1,)),
        ],
        compiler_params=pltpu.CompilerParams(collective_id=0, has_side_effects=True, vmem_limit_bytes=60 << 20),
    )(
        reach_pre, jnp.swapaxes(strategy, 1, 2), ranks, jnp.transpose(boards, (2, 0, 1)),
        pot, line_act, jnp.asarray(card_rows()), river_live, iso_weight,
    )


def solution(mesh):
    in_specs = (
        P(("board", "hand")),
        P("board", None, "hand"),
        P("board", None, None),
        P("board", None, None),
        P("board"),
        P("board"),
        P(),
        P(),
    )
    return jax.shard_map(body, mesh=mesh, in_specs=in_specs, out_specs=P("hand"), check_vma=False)
```

```python
import functools

import jax
import jax.numpy as jnp
import numpy as np
from jax import lax
from jax.experimental import pallas as pl
from jax.experimental.pallas import tpu as pltpu
from jax.sharding import PartitionSpec as P

HANDS = 1326
HPAD = 1408
RIV = 8
LINES = 128
ACTS = 3
NF = 8
OWN = 352
OPAD = 384
CHUNK = 11
DEAD = 128.0
ZS, NB = 4, 32
PARTS = 3
ROWS = PARTS * ACTS * NF
RPAD = 80
HALF = NF // 2
KPAD = ZS * OPAD
STEP = 128
TOP = 96
SPLIT = (3, 6)
f32, bf16, f8 = jnp.float32, jnp.bfloat16, jnp.float8_e4m3fn


def card_rows():
    first, second = np.triu_indices(52, 1)
    padding = HPAD - HANDS
    rows = np.zeros((ZS, 8, OPAD), np.float32)
    rows[:, 0], rows[:, 1] = 52, 53
    rows[:, 0, :OWN] = np.concatenate([first, np.full(padding, 52)]).reshape(ZS, OWN)
    rows[:, 1, :OWN] = np.concatenate([second, np.full(padding, 53)]).reshape(ZS, OWN)
    rows[:, 2, :OWN] = (np.arange(HPAD) < HANDS).reshape(ZS, OWN)
    return rows


def pieces(value):
    high = value.astype(bf16)
    rest = value - high.astype(f32)
    middle = rest.astype(bf16)
    low = (rest - middle.astype(f32)).astype(bf16)
    return high, middle, low


def kernel(
    reach_hbm, strategy_hbm, ranks_hbm, boards_hbm, pot_hbm, act_hbm, cards_hbm, live_hbm, iso_hbm,
    out_ref,
    reach_in, strat, ranks, boards, pot, act, cards, live_smem, iso_smem,
    quarters, rel, inc, lhs, slots, onehot, block, mat, sel, spots, scales, wslot, sums, gathered, parts, final,
    load_sem, s1, r1, s2, r2, s3, r3, s4, r4, s5, r5,
):
    board, hand = lax.axis_index("board"), lax.axis_index("hand")
    plane_ids = [(board + k) % NB for k in range(1, NB)]

    reach_load = pltpu.make_async_copy(reach_hbm, reach_in, load_sem.at[0])
    reach_load.start()
    barrier = pltpu.get_barrier_semaphore()

    def greet(b, h):
        pl.semaphore_signal(barrier, inc=1, device_id=(b, h), device_id_type=pl.DeviceIdType.MESH)

    for b in plane_ids:
        greet(b, hand)
    for k in (2, 1, 3):
        greet(board, (hand + k) % ZS)

    loads = [
        pltpu.make_async_copy(a, b, load_sem.at[i + 1])
        for i, (a, b) in enumerate(
            [(cards_hbm, cards), (boards_hbm, boards), (live_hbm, live_smem), (iso_hbm, iso_smem),
             (ranks_hbm, ranks), (pot_hbm, pot), (act_hbm, act), (strategy_hbm, strat)]
        )
    ]
    for c in loads:
        c.start()
    reach_load.wait()
    gathered[pl.ds(hand, 1), pl.ds(board, 1), 0:1, 0:CHUNK] = reach_in[...].reshape(1, 1, 1, CHUNK)

    def remote(src, dst, send, recv, b, h):
        return pltpu.make_async_remote_copy(
            src_ref=src, dst_ref=dst, send_sem=send, recv_sem=recv,
            device_id=(b, h), device_id_type=pl.DeviceIdType.MESH,
        )

    pl.semaphore_wait(barrier, NB - 1 + ZS - 1)
    row = gathered.at[hand, pl.ds(board, 1)]
    first = [remote(row, row, s1.at[i], r1.at[i], b, hand) for i, b in enumerate(plane_ids)]
    for c in first:
        c.start()
    for c in loads[:5]:
        c.wait()

    runout = lax.broadcasted_iota(jnp.int32, (RIV, 1), 0)
    diagonal = lax.broadcasted_iota(jnp.int32, (RIV, RIV), 0) == lax.broadcasted_iota(jnp.int32, (RIV, RIV), 1)
    for f in range(NF):
        drawn = []
        for k in range(5):
            card = jnp.broadcast_to(boards[k, f].astype(f32).reshape(1, RIV), (RIV, RIV))
            drawn.append(jnp.sum(jnp.where(diagonal, card, 0.0), axis=1, keepdims=True))
        beyond = runout >= live_smem[f]
        for z in range(ZS):
            if z < ZS - 1:
                part = ranks[f, :, OWN * z : OWN * z + OPAD].astype(f32)
            else:
                part = jnp.concatenate([ranks[f, :, OWN * z :].astype(f32), jnp.zeros((RIV, OPAD - OWN), f32)], axis=1)
            dead = (cards[z, 2:3, :] < 0.5) | beyond
            for card in drawn:
                dead = dead | (cards[z, 0:1, :] == card) | (cards[z, 1:2, :] == card)
            quarters[z, RIV * f : RIV * (f + 1), :] = jnp.where(dead, DEAD, part)
    card_id = lax.broadcasted_iota(jnp.int32, (128, OPAD), 0).astype(f32)
    for z in range(ZS):
        inc[z] = ((card_id == cards[z, 0:1, :]) | (card_id == cards[z, 1:2, :])).astype(f32)

    for k in range(ZS):
        rel[:, OPAD * k : OPAD * (k + 1)] = quarters[(hand + ZS - k) % ZS]
    own = quarters[hand]
    alive = (own < DEAD).astype(f32)
    ranked = own * alive
    both = [t for f in range(NF) for t in (ranked[RIV * f : RIV * (f + 1)], alive[RIV * f : RIV * (f + 1)])]
    lhs[...] = jnp.concatenate(both, axis=0).T[0:OWN].astype(bf16)
    held_cards = inc[hand].T[0:OWN].astype(bf16)
    for k in range(ZS):
        shared = jnp.dot(held_cards, inc[(hand + ZS - k) % ZS].astype(bf16), preferred_element_type=f32)
        block[:, OPAD * k : OPAD * (k + 1)] = jnp.where(shared > 0.5, 0.0, 1.0).astype(bf16)

    slots[...] = jnp.zeros(slots.shape, bf16)
    at = lax.broadcasted_iota(jnp.int32, (2 * RIV, RIV * STEP), 1)
    which = lax.broadcasted_iota(jnp.int32, (2 * RIV, RIV * STEP), 0)
    pattern = jnp.where(which < RIV, 1.0, -(at % STEP).astype(f32))
    slots[112:128, :] = jnp.where(at // STEP == which % RIV, pattern, 0.0).astype(bf16)
    for r in range(RIV):
        onehot[STEP * r + TOP : STEP * (r + 1), :] = jnp.zeros((STEP - TOP, KPAD), bf16).astype(f8)
    slot = lax.broadcasted_iota(jnp.int32, (TOP, KPAD), 0).astype(f32).astype(bf16)
    one, zero = jnp.ones((), bf16), jnp.zeros((), bf16)

    def build(lo, hi):
        def step(f, carry):
            pick = slots[pl.ds(pl.multiple_of(112 - 16 * f, 16), 128), :]
            beats = jnp.dot(lhs[...], pick, preferred_element_type=f32)
            beats = jnp.maximum(jnp.minimum(beats, 1.0), -1.0).astype(bf16).astype(f8)
            for r in range(RIV):
                ranked = jnp.broadcast_to(rel[pl.ds(RIV * f + r, 1), :], (TOP, KPAD)).astype(bf16)
                onehot[STEP * r : STEP * r + TOP, :] = jnp.where(slot == ranked, one, zero).astype(f8)
            net = jnp.dot(beats, onehot[...], preferred_element_type=f32)
            for k in range(ZS):
                here = net[:, OPAD * k : OPAD * (k + 1)].astype(bf16) * block[:, OPAD * k : OPAD * (k + 1)]
                start = ((f // HALF) * ZS + k) * HALF * OPAD + (f % HALF) * OPAD
                mat[:, pl.ds(pl.multiple_of(start, 128), OPAD)] = here
            return carry

        lax.fori_loop(lo, hi, step, 0)

    for c in loads[5:7]:
        c.wait()
    lines_row = lax.broadcasted_iota(jnp.int32, (HALF, LINES), 0)
    pot_row, act_row = pot[...].reshape(1, LINES), act[...].reshape(1, LINES)
    weights = [pieces(jnp.where(act_row == a, pot_row, 0.0)) for a in range(ACTS)]
    for f in range(HALF):
        groups = [
            jnp.where(lines_row == f, jnp.broadcast_to(weights[a][p].astype(f32), (HALF, LINES)), 0.0)
            for p in range(PARTS) for a in range(ACTS)
        ] + [jnp.zeros((HALF, LINES), f32)]
        sel[f] = jnp.concatenate(groups, axis=0).astype(bf16)

    flop_id = lax.broadcasted_iota(jnp.int32, (NF, OPAD), 0)
    scale = jnp.zeros((NF, OPAD), f32)
    weight = jnp.float32(0)
    for f in range(NF):
        iso = iso_smem[f].astype(f32)
        weight += iso
        scale = jnp.where(flop_id == f, iso / live_smem[f].astype(f32), scale)
    scales[0] = scale
    scales[1] = jnp.full((NF, OPAD), weight)

    at_hand = lax.broadcasted_iota(jnp.int32, (OWN, 128), 0)
    at_lane = lax.broadcasted_iota(jnp.int32, (OWN, 128), 1)
    chunk = at_hand // CHUNK
    place = (chunk % ZS) * 8 + chunk // ZS
    spots[...] = ((at_lane % 32 == place) & (at_lane < 96)).astype(f32).astype(bf16)

    build(0, SPLIT[0])
    for c in first:
        c.wait_recv()
    second = []
    for k in (2, 1, 3):
        rows_of = gathered.at[hand, pl.ds(((hand + k) % ZS) * 8, 8)]
        second.append(remote(rows_of, rows_of, s2.at[k - 1], r2.at[k - 1], board, (hand + k) % ZS))
    for c in second:
        c.start()
    plane = gathered[pl.ds(hand, 1), :, 0, :].reshape(NB, 128)
    lane = lax.broadcasted_iota(jnp.int32, (NB, 128), 1)
    entry = (lax.broadcasted_iota(jnp.int32, (NB, 128), 0) * ZS + hand) * CHUNK + lane
    plane = jnp.where((lane < CHUNK) & (entry < HANDS), plane, 0.0)
    parts[pl.ds(hand, 1)] = jnp.sum(plane, axis=0, keepdims=True)[None]
    part = parts.at[pl.ds(hand, 1)]
    third = [remote(part, part, s3.at[k - 1], r3.at[k - 1], board, (hand + k) % ZS) for k in (2, 1, 3)]
    for c in third:
        c.start()
    build(SPLIT[0], SPLIT[1])
    loads[7].wait()
    for c in second + third:
        c.wait_recv()

    total = jnp.sum(jnp.sum(parts[...], axis=0))
    quarter = jnp.concatenate([gathered[z, pl.ds(hand * 8, 8), 0, :] for z in range(ZS)], axis=0)
    stacked = jnp.concatenate([p.astype(f32) for p in pieces(quarter / total)] + [jnp.zeros((32, 128), f32)], axis=0)
    laid = jnp.dot(spots[...], stacked.astype(bf16), preferred_element_type=f32)
    share = jnp.sum(jnp.where(at_lane == at_hand - chunk * CHUNK, laid, 0.0), axis=1, keepdims=True)

    sent = []
    for h in range(2):
        summed = jnp.zeros((40, OWN), f32)
        for f in range(HALF):
            lines = (strat[HALF * h + f].astype(f32) * share).astype(bf16)
            summed += lax.dot_general(sel[f], lines, (((1,), (1,)), ((), ())), preferred_element_type=f32)
        summed = jnp.concatenate([summed, jnp.zeros((40, OPAD - OWN), f32)], axis=1)
        acts = summed[0:12] + summed[12:24] + summed[24:36]
        for a in range(ACTS):
            wslot[pl.ds(hand, 1), h, a] = acts[HALF * a : HALF * (a + 1)][None]
        held = wslot.at[pl.ds(hand, 1), h]
        sent.append([
            remote(held, held, s4.at[3 * h + k - 1], r4.at[3 * h + k - 1], board, (hand + k) % ZS) for k in (2, 1, 3)
        ])
        for c in sent[h]:
            c.start()
    build(SPLIT[1], NF)

    flop_of_lane = lax.broadcasted_iota(jnp.int32, (NF, OPAD), 0)

    def times_reach(h, k):
        cut = [p.astype(f32) for p in pieces(wslot[(hand + ZS - k) % ZS, h])]
        columns = []
        for f in range(HALF):
            groups = [
                jnp.where(flop_of_lane == HALF * h + f, cut[p][a, f : f + 1], 0.0)
                for p in range(PARTS) for a in range(ACTS)
            ] + [jnp.zeros((NF, OPAD), f32)]
            columns.append(jnp.concatenate(groups, axis=0).astype(bf16))
        return columns

    def product(h, ks):
        right = jnp.concatenate([c for k in ks for c in times_reach(h, k)], axis=1)
        start = (h * ZS + ks[0]) * HALF * OPAD
        left = mat[:, start : start + len(ks) * HALF * OPAD]
        return lax.dot_general(left, right, (((1,), (1,)), ((), ())), preferred_element_type=f32)

    sums[...] = jnp.zeros((OWN, RPAD), f32)
    sums[...] += product(0, (0,))
    sums[...] += product(1, (0,))
    for h in range(2):
        for c in sent[h]:
            c.wait_recv()
        sums[...] += product(h, (1, 2, 3))
    values = sums[...]
    values = jnp.concatenate([values, jnp.zeros((OWN, 128 - RPAD), f32)], axis=1)
    values = jnp.concatenate([values, jnp.zeros((OPAD - OWN, 128), f32)], axis=0).T
    best = None
    for a in range(ACTS):
        acted = sum(values[(p * ACTS + a) * NF : (p * ACTS + a + 1) * NF] for p in range(PARTS))
        best = acted if best is None else jnp.maximum(best, acted)
    partial = jnp.sum(best * scales[0], axis=0, keepdims=True)
    partial = jnp.where(lax.broadcasted_iota(jnp.int32, (1, OPAD), 1) == OWN, scales[1, 0:1], partial)
    final[pl.ds(board, 1)] = partial[None]
    ours = final.at[pl.ds(board, 1)]
    fifth = [remote(ours, ours, s5.at[i], r5.at[i], b, hand) for i, b in enumerate(plane_ids)]
    for c in fifth:
        c.start()
    for c in fifth:
        c.wait_recv()
    whole = jnp.sum(final[...], axis=0)
    out_ref[...] = (whole[:, 0:OWN] / whole[:, OWN : OWN + 1]).reshape(OWN)
    for c in first + second + third + sent[0] + sent[1] + fifth:
        c.wait_send()


def body(reach_pre, strategy, ranks, boards, river_live, iso_weight, pot, line_act):
    anywhere = pl.BlockSpec(memory_space=pl.ANY)
    dma = pltpu.SemaphoreType.DMA
    return pl.pallas_call(
        kernel,
        out_shape=jax.ShapeDtypeStruct((OWN,), f32),
        in_specs=[anywhere] * 9,
        out_specs=pl.BlockSpec(memory_space=pltpu.VMEM),
        scratch_shapes=[
            pltpu.VMEM((CHUNK,), f32),
            pltpu.VMEM((NF, OWN, LINES), bf16),
            pltpu.VMEM((NF, RIV, HPAD), jnp.int32),
            pltpu.VMEM((5, NF, RIV), jnp.int32),
            pltpu.VMEM((LINES,), f32),
            pltpu.VMEM((LINES,), jnp.int32),
            pltpu.VMEM((ZS, 8, OPAD), f32),
            pltpu.SMEM((NF,), jnp.int32),
            pltpu.SMEM((NF,), jnp.int32),
            pltpu.VMEM((ZS, NF * RIV, OPAD), f32),
            pltpu.VMEM((NF * RIV, KPAD), f32),
            pltpu.VMEM((ZS, 128, OPAD), f32),
            pltpu.VMEM((OWN, 128), bf16),
            pltpu.VMEM((256, RIV * STEP), bf16),
            pltpu.VMEM((RIV * STEP, KPAD), f8),
            pltpu.VMEM((OWN, KPAD), bf16),
            pltpu.VMEM((OWN, NF * KPAD), bf16),
            pltpu.VMEM((HALF, 40, LINES), bf16),
            pltpu.VMEM((OWN, 128), bf16),
            pltpu.VMEM((2, NF, OPAD), f32),
            pltpu.VMEM((ZS, 2, ACTS, HALF, OPAD), f32),
            pltpu.VMEM((OWN, RPAD), f32),
            pltpu.VMEM((ZS, NB, 1, 128), f32),
            pltpu.VMEM((ZS, 1, 128), f32),
            pltpu.VMEM((NB, 1, OPAD), f32),
            dma((9,)), dma((NB - 1,)), dma((NB - 1,)), dma((3,)), dma((3,)), dma((3,)), dma((3,)), dma((6,)), dma((6,)),
            dma((NB - 1,)), dma((NB - 1,)),
        ],
        compiler_params=pltpu.CompilerParams(collective_id=0, has_side_effects=True, vmem_limit_bytes=60 << 20),
    )(
        reach_pre, jnp.swapaxes(strategy, 1, 2), ranks, jnp.transpose(boards, (2, 0, 1)),
        pot, line_act, jnp.asarray(card_rows()), river_live, iso_weight,
    )


def solution(mesh):
    in_specs = (
        P(("board", "hand")),
        P("board", None, "hand"),
        P("board", None, None),
        P("board", None, None),
        P("board"),
        P("board"),
        P(),
        P(),
    )
    return jax.shard_map(body, mesh=mesh, in_specs=in_specs, out_specs=P("hand"), check_vma=False)
```

```python
import functools

import jax
import jax.numpy as jnp
import numpy as np
from jax import lax
from jax.experimental import pallas as pl
from jax.experimental.pallas import tpu as pltpu
from jax.sharding import PartitionSpec as P

HANDS = 1326
HPAD = 1408
RIV = 8
LINES = 128
ACTS = 3
NF = 8
OWN = 352
OPAD = 384
CHUNK = 11
DEAD = 128.0
ZS, NB = 4, 32
PARTS = 3
ROWS = PARTS * ACTS * NF
RPAD = 72
HALF = NF // 2
KPAD = ZS * OPAD
STEP = 128
TOP = 96
SPLIT = (3, 6)
f32, bf16, f8 = jnp.float32, jnp.bfloat16, jnp.float8_e4m3fn


def card_rows():
    first, second = np.triu_indices(52, 1)
    padding = HPAD - HANDS
    rows = np.zeros((ZS, 8, OPAD), np.float32)
    rows[:, 0], rows[:, 1] = 52, 53
    rows[:, 0, :OWN] = np.concatenate([first, np.full(padding, 52)]).reshape(ZS, OWN)
    rows[:, 1, :OWN] = np.concatenate([second, np.full(padding, 53)]).reshape(ZS, OWN)
    rows[:, 2, :OWN] = (np.arange(HPAD) < HANDS).reshape(ZS, OWN)
    return rows


def pieces(value):
    high = value.astype(bf16)
    rest = value - high.astype(f32)
    middle = rest.astype(bf16)
    low = (rest - middle.astype(f32)).astype(bf16)
    return high, middle, low


def kernel(
    reach_hbm, strategy_hbm, ranks_hbm, boards_hbm, pot_hbm, act_hbm, cards_hbm, live_hbm, iso_hbm,
    out_ref,
    reach_in, strat, ranks, boards, pot, act, cards, live_smem, iso_smem,
    quarters, rel, inc, lhs, slots, onehot, block, mat, sel, spots, scales, wslot, sums, gathered, parts, final,
    load_sem, s1, r1, s2, r2, s3, r3, s4, r4, s5, r5,
):
    board, hand = lax.axis_index("board"), lax.axis_index("hand")
    plane_ids = [(board + k) % NB for k in range(1, NB)]

    reach_load = pltpu.make_async_copy(reach_hbm, reach_in, load_sem.at[0])
    reach_load.start()
    barrier = pltpu.get_barrier_semaphore()

    def greet(b, h):
        pl.semaphore_signal(barrier, inc=1, device_id=(b, h), device_id_type=pl.DeviceIdType.MESH)

    for b in plane_ids:
        greet(b, hand)
    for k in (2, 1, 3):
        greet(board, (hand + k) % ZS)

    loads = [
        pltpu.make_async_copy(a, b, load_sem.at[i + 1])
        for i, (a, b) in enumerate(
            [(cards_hbm, cards), (boards_hbm, boards), (live_hbm, live_smem), (iso_hbm, iso_smem),
             (ranks_hbm, ranks), (pot_hbm, pot), (act_hbm, act), (strategy_hbm, strat)]
        )
    ]
    for c in loads:
        c.start()
    reach_load.wait()
    gathered[pl.ds(hand, 1), pl.ds(board, 1), 0:1, 0:CHUNK] = reach_in[...].reshape(1, 1, 1, CHUNK)

    def remote(src, dst, send, recv, b, h):
        return pltpu.make_async_remote_copy(
            src_ref=src, dst_ref=dst, send_sem=send, recv_sem=recv,
            device_id=(b, h), device_id_type=pl.DeviceIdType.MESH,
        )

    pl.semaphore_wait(barrier, NB - 1 + ZS - 1)
    row = gathered.at[hand, pl.ds(board, 1)]
    first = [remote(row, row, s1.at[i], r1.at[i], b, hand) for i, b in enumerate(plane_ids)]
    for c in first:
        c.start()
    for c in loads[:5]:
        c.wait()

    runout = lax.broadcasted_iota(jnp.int32, (RIV, 1), 0)
    diagonal = lax.broadcasted_iota(jnp.int32, (RIV, RIV), 0) == lax.broadcasted_iota(jnp.int32, (RIV, RIV), 1)
    for f in range(NF):
        drawn = []
        for k in range(5):
            card = jnp.broadcast_to(boards[k, f].astype(f32).reshape(1, RIV), (RIV, RIV))
            drawn.append(jnp.sum(jnp.where(diagonal, card, 0.0), axis=1, keepdims=True))
        beyond = runout >= live_smem[f]
        for z in range(ZS):
            if z < ZS - 1:
                part = ranks[f, :, OWN * z : OWN * z + OPAD].astype(f32)
            else:
                part = jnp.concatenate([ranks[f, :, OWN * z :].astype(f32), jnp.zeros((RIV, OPAD - OWN), f32)], axis=1)
            dead = (cards[z, 2:3, :] < 0.5) | beyond
            for card in drawn:
                dead = dead | (cards[z, 0:1, :] == card) | (cards[z, 1:2, :] == card)
            quarters[z, RIV * f : RIV * (f + 1), :] = jnp.where(dead, DEAD, part)
    card_id = lax.broadcasted_iota(jnp.int32, (128, OPAD), 0).astype(f32)
    for z in range(ZS):
        inc[z] = ((card_id == cards[z, 0:1, :]) | (card_id == cards[z, 1:2, :])).astype(f32)

    for k in range(ZS):
        rel[:, OPAD * k : OPAD * (k + 1)] = quarters[(hand + ZS - k) % ZS]
    own = quarters[hand]
    alive = (own < DEAD).astype(f32)
    ranked = own * alive
    both = [t for f in range(NF) for t in (ranked[RIV * f : RIV * (f + 1)], alive[RIV * f : RIV * (f + 1)])]
    lhs[...] = jnp.concatenate(both, axis=0).T[0:OWN].astype(bf16)
    held_cards = inc[hand].T[0:OWN].astype(bf16)
    for k in range(ZS):
        shared = jnp.dot(held_cards, inc[(hand + ZS - k) % ZS].astype(bf16), preferred_element_type=f32)
        block[:, OPAD * k : OPAD * (k + 1)] = jnp.where(shared > 0.5, 0.0, 1.0).astype(bf16)

    slots[...] = jnp.zeros(slots.shape, bf16)
    at = lax.broadcasted_iota(jnp.int32, (2 * RIV, RIV * STEP), 1)
    which = lax.broadcasted_iota(jnp.int32, (2 * RIV, RIV * STEP), 0)
    pattern = jnp.where(which < RIV, 1.0, -(at % STEP).astype(f32))
    slots[112:128, :] = jnp.where(at // STEP == which % RIV, pattern, 0.0).astype(bf16)
    for r in range(RIV):
        onehot[STEP * r + TOP : STEP * (r + 1), :] = jnp.zeros((STEP - TOP, KPAD), bf16).astype(f8)
    slot = lax.broadcasted_iota(jnp.int32, (TOP, KPAD), 0).astype(f32).astype(bf16)
    one, zero = jnp.ones((), bf16), jnp.zeros((), bf16)

    def build(lo, hi):
        def step(f, carry):
            pick = slots[pl.ds(pl.multiple_of(112 - 16 * f, 16), 128), :]
            beats = jnp.dot(lhs[...], pick, preferred_element_type=f32)
            beats = jnp.maximum(jnp.minimum(beats, 1.0), -1.0).astype(bf16).astype(f8)
            for r in range(RIV):
                ranked = jnp.broadcast_to(rel[pl.ds(RIV * f + r, 1), :], (TOP, KPAD)).astype(bf16)
                onehot[STEP * r : STEP * r + TOP, :] = jnp.where(slot == ranked, one, zero).astype(f8)
            net = jnp.dot(beats, onehot[...], preferred_element_type=f32)
            for k in range(ZS):
                here = net[:, OPAD * k : OPAD * (k + 1)].astype(bf16) * block[:, OPAD * k : OPAD * (k + 1)]
                start = ((f // HALF) * ZS + k) * HALF * OPAD + (f % HALF) * OPAD
                mat[:, pl.ds(pl.multiple_of(start, 128), OPAD)] = here
            return carry

        lax.fori_loop(lo, hi, step, 0)

    for c in loads[5:7]:
        c.wait()
    lines_row = lax.broadcasted_iota(jnp.int32, (HALF, LINES), 0)
    pot_row, act_row = pot[...].reshape(1, LINES), act[...].reshape(1, LINES)
    weights = [pieces(jnp.where(act_row == a, pot_row, 0.0)) for a in range(ACTS)]
    for f in range(HALF):
        groups = [
            jnp.where(lines_row == f, jnp.broadcast_to(weights[a][p].astype(f32), (HALF, LINES)), 0.0)
            for p in range(PARTS) for a in range(ACTS)
        ] + [jnp.zeros((HALF, LINES), f32)]
        sel[f] = jnp.concatenate(groups, axis=0).astype(bf16)

    flop_id = lax.broadcasted_iota(jnp.int32, (NF, OPAD), 0)
    scale = jnp.zeros((NF, OPAD), f32)
    weight = jnp.float32(0)
    for f in range(NF):
        iso = iso_smem[f].astype(f32)
        weight += iso
        scale = jnp.where(flop_id == f, iso / live_smem[f].astype(f32), scale)
    scales[0] = scale
    scales[1] = jnp.full((NF, OPAD), weight)

    at_hand = lax.broadcasted_iota(jnp.int32, (OWN, 128), 0)
    at_lane = lax.broadcasted_iota(jnp.int32, (OWN, 128), 1)
    chunk = at_hand // CHUNK
    place = (chunk % ZS) * 8 + chunk // ZS
    spots[...] = ((at_lane % 32 == place) & (at_lane < 96)).astype(f32).astype(bf16)

    build(0, SPLIT[0])
    for c in first:
        c.wait_recv()
    second = []
    for k in (2, 1, 3):
        rows_of = gathered.at[hand, pl.ds(((hand + k) % ZS) * 8, 8)]
        second.append(remote(rows_of, rows_of, s2.at[k - 1], r2.at[k - 1], board, (hand + k) % ZS))
    for c in second:
        c.start()
    plane = gathered[pl.ds(hand, 1), :, 0, :].reshape(NB, 128)
    lane = lax.broadcasted_iota(jnp.int32, (NB, 128), 1)
    entry = (lax.broadcasted_iota(jnp.int32, (NB, 128), 0) * ZS + hand) * CHUNK + lane
    plane = jnp.where((lane < CHUNK) & (entry < HANDS), plane, 0.0)
    parts[pl.ds(hand, 1)] = jnp.sum(plane, axis=0, keepdims=True)[None]
    part = parts.at[pl.ds(hand, 1)]
    third = [remote(part, part, s3.at[k - 1], r3.at[k - 1], board, (hand + k) % ZS) for k in (2, 1, 3)]
    for c in third:
        c.start()
    build(SPLIT[0], SPLIT[1])
    loads[7].wait()
    for c in second + third:
        c.wait_recv()

    total = jnp.sum(jnp.sum(parts[...], axis=0))
    quarter = jnp.concatenate([gathered[z, pl.ds(hand * 8, 8), 0, :] for z in range(ZS)], axis=0)
    stacked = jnp.concatenate([p.astype(f32) for p in pieces(quarter / total)] + [jnp.zeros((32, 128), f32)], axis=0)
    laid = jnp.dot(spots[...], stacked.astype(bf16), preferred_element_type=f32)
    share = jnp.sum(jnp.where(at_lane == at_hand - chunk * CHUNK, laid, 0.0), axis=1, keepdims=True)

    sent = []
    for h in range(2):
        summed = jnp.zeros((40, OWN), f32)
        for f in range(HALF):
            lines = (strat[HALF * h + f].astype(f32) * share).astype(bf16)
            summed += lax.dot_general(sel[f], lines, (((1,), (1,)), ((), ())), preferred_element_type=f32)
        summed = jnp.concatenate([summed, jnp.zeros((40, OPAD - OWN), f32)], axis=1)
        acts = summed[0:12] + summed[12:24] + summed[24:36]
        for a in range(ACTS):
            wslot[pl.ds(hand, 1), h, a] = acts[HALF * a : HALF * (a + 1)][None]
        held = wslot.at[pl.ds(hand, 1), h]
        sent.append([
            remote(held, held, s4.at[3 * h + k - 1], r4.at[3 * h + k - 1], board, (hand + k) % ZS) for k in (2, 1, 3)
        ])
        for c in sent[h]:
            c.start()
    build(SPLIT[1], NF)

    flop_of_lane = lax.broadcasted_iota(jnp.int32, (NF, OPAD), 0)

    def times_reach(h, k):
        cut = [p.astype(f32) for p in pieces(wslot[(hand + ZS - k) % ZS, h])]
        columns = []
        for f in range(HALF):
            groups = [
                jnp.where(flop_of_lane == HALF * h + f, cut[p][a, f : f + 1], 0.0)
                for p in range(PARTS) for a in range(ACTS)
            ]
            columns.append(jnp.concatenate(groups, axis=0).astype(bf16))
        return columns

    def product(h, ks):
        right = jnp.concatenate([c for k in ks for c in times_reach(h, k)], axis=1)
        start = (h * ZS + ks[0]) * HALF * OPAD
        left = mat[:, start : start + len(ks) * HALF * OPAD]
        return lax.dot_general(left, right, (((1,), (1,)), ((), ())), preferred_element_type=f32)

    sums[...] = jnp.zeros((OWN, RPAD), f32)
    sums[...] += product(0, (0,))
    sums[...] += product(1, (0,))
    for h in range(2):
        for c in sent[h]:
            c.wait_recv()
        sums[...] += product(h, (1, 2, 3))
    values = sums[...]
    values = jnp.concatenate([values, jnp.zeros((OWN, 128 - RPAD), f32)], axis=1)
    values = jnp.concatenate([values, jnp.zeros((OPAD - OWN, 128), f32)], axis=0).T
    best = None
    for a in range(ACTS):
        acted = sum(values[(p * ACTS + a) * NF : (p * ACTS + a + 1) * NF] for p in range(PARTS))
        best = acted if best is None else jnp.maximum(best, acted)
    partial = jnp.sum(best * scales[0], axis=0, keepdims=True)
    partial = jnp.where(lax.broadcasted_iota(jnp.int32, (1, OPAD), 1) == OWN, scales[1, 0:1], partial)
    final[pl.ds(board, 1)] = partial[None]
    ours = final.at[pl.ds(board, 1)]
    fifth = [remote(ours, ours, s5.at[i], r5.at[i], b, hand) for i, b in enumerate(plane_ids)]
    for c in fifth:
        c.start()
    for c in fifth:
        c.wait_recv()
    whole = jnp.sum(final[...], axis=0)
    out_ref[...] = (whole[:, 0:OWN] / whole[:, OWN : OWN + 1]).reshape(OWN)
    for c in first + second + third + sent[0] + sent[1] + fifth:
        c.wait_send()


def body(reach_pre, strategy, ranks, boards, river_live, iso_weight, pot, line_act):
    anywhere = pl.BlockSpec(memory_space=pl.ANY)
    dma = pltpu.SemaphoreType.DMA
    return pl.pallas_call(
        kernel,
        out_shape=jax.ShapeDtypeStruct((OWN,), f32),
        in_specs=[anywhere] * 9,
        out_specs=pl.BlockSpec(memory_space=pltpu.VMEM),
        scratch_shapes=[
            pltpu.VMEM((CHUNK,), f32),
            pltpu.VMEM((NF, OWN, LINES), bf16),
            pltpu.VMEM((NF, RIV, HPAD), jnp.int32),
            pltpu.VMEM((5, NF, RIV), jnp.int32),
            pltpu.VMEM((LINES,), f32),
            pltpu.VMEM((LINES,), jnp.int32),
            pltpu.VMEM((ZS, 8, OPAD), f32),
            pltpu.SMEM((NF,), jnp.int32),
            pltpu.SMEM((NF,), jnp.int32),
            pltpu.VMEM((ZS, NF * RIV, OPAD), f32),
            pltpu.VMEM((NF * RIV, KPAD), f32),
            pltpu.VMEM((ZS, 128, OPAD), f32),
            pltpu.VMEM((OWN, 128), bf16),
            pltpu.VMEM((256, RIV * STEP), bf16),
            pltpu.VMEM((RIV * STEP, KPAD), f8),
            pltpu.VMEM((OWN, KPAD), bf16),
            pltpu.VMEM((OWN, NF * KPAD), bf16),
            pltpu.VMEM((HALF, 40, LINES), bf16),
            pltpu.VMEM((OWN, 128), bf16),
            pltpu.VMEM((2, NF, OPAD), f32),
            pltpu.VMEM((ZS, 2, ACTS, HALF, OPAD), f32),
            pltpu.VMEM((OWN, RPAD), f32),
            pltpu.VMEM((ZS, NB, 1, 128), f32),
            pltpu.VMEM((ZS, 1, 128), f32),
            pltpu.VMEM((NB, 1, OPAD), f32),
            dma((9,)), dma((NB - 1,)), dma((NB - 1,)), dma((3,)), dma((3,)), dma((3,)), dma((3,)), dma((6,)), dma((6,)),
            dma((NB - 1,)), dma((NB - 1,)),
        ],
        compiler_params=pltpu.CompilerParams(collective_id=0, has_side_effects=True, vmem_limit_bytes=60 << 20),
    )(
        reach_pre, jnp.swapaxes(strategy, 1, 2), ranks, jnp.transpose(boards, (2, 0, 1)),
        pot, line_act, jnp.asarray(card_rows()), river_live, iso_weight,
    )


def solution(mesh):
    in_specs = (
        P(("board", "hand")),
        P("board", None, "hand"),
        P("board", None, None),
        P("board", None, None),
        P("board"),
        P("board"),
        P(),
        P(),
    )
    return jax.shard_map(body, mesh=mesh, in_specs=in_specs, out_specs=P("hand"), check_vma=False)
```
